32 devices in a mesh: groups: 2 (over y), seq: 4 (over z), head: 2 (over x), sub: 2 (over core).
Axes of the slice: x: 2, y: 2, z: 4, core: 2. Of those that a mesh axis runs over, the one named last changes fastest.
Arguments:
- queries: bfloat16 [128, 128, 16, 128], P(('groups', 'seq'), None, ('head', 'sub')), parts along dimension 0, may hold values from -6 to 6
- keys: bfloat16 [128, 128, 16, 128], P(('groups', 'seq'), None, ('head', 'sub')), parts along dimension 0, may hold values from -6 to 6
- values: bfloat16 [128, 128, 16, 2, 128], P(('groups', 'seq'), None, ('head', 'sub')), parts along dimension 0, may hold values from -6 to 6
- log_decay: bfloat16 [128, 128, 16, 2], P(('groups', 'seq'), None, ('head', 'sub')), parts along dimension 0, may hold values from -0.8 to 0
- write_rate: bfloat16 [128, 128, 16, 2], P(('groups', 'seq'), None, ('head', 'sub')), parts along dimension 0, may hold values from 0.049804688 to 0.94921875
- norm_gain: bfloat16 [128], replicated, may hold values from 0.25 to 1.75
- parent_cache: float32 [32, 16, 2, 128, 128], P(('groups', 'seq'), ('head', 'sub')), parts along dimension 0, may hold values from -3 to 3
- order: int32 [128], P('groups'), parts along dimension 0, may hold values from 0 to 63, as said below
- parent_owner: int32 [128], P('groups'), parts along dimension 0, may hold values from 0 to 3, as said below
- parent_slot: int32 [128], P('groups'), parts along dimension 0, may hold values from 0 to 3
- token_count: int32 [128], P('groups'), parts along dimension 0, may hold values from 64 to 128, as said below
Outputs:
- mixed: bfloat16 [128, 128, 16, 2, 128], P(('groups', 'seq'), None, ('head', 'sub')), parts along dimension 0
- final_state: float32 [128, 16, 2, 128, 128], P(('groups', 'seq'), ('head', 'sub')), parts along dimension 0
The draws below stay inside these ranges and needn't reach their ends.
There are 2 independent parts, one for each index of `groups`. The reference program is written for one: setup_inputs(seed, part) draws one part's arguments, and reference() takes and returns one part's arrays. A program takes and returns all parts, laid end to end along the dimension named above; an argument that names none is the same for every part. Nothing has to cross between parts.
Inputs may be any that keep to these rules, and one draw needn't show every extreme that they name: A permutation; slot j = p * 16 + s * 4 + r with r < 4 is processed by seq device p and holds an expansion that arrives on seq device s, so order[j] // 16 = s. `parent_owner`: among the 16 expansions processed by one seq device at most 8 have their parent on one owner, and on some device exactly 8 do. `token_count`: multiples of 64; some expansion has 128 and some has 64.
All inputs are finite; a program needn't handle non-finite values.
Results may differ from the reference program's by a relative error of at most 0.001.
Values may be sent and summed in bfloat16 or wider, within the bound.
A program may use at most 192 MiB of HBM per device.

```python
import jax
import jax.numpy as jnp
from jax import lax

KEY_HEAD_COUNT = 16
DK = 128
DV = 128
TOKEN_SLOTS = 128
SPAN = 64
EXP_DEV = 16
PAR_DEV = 4
GROUP_EXPANSIONS = 64
PARENTS = 16
CAP = 8
N_SEQ = 4


def owner_plan(key):
    key_perm, key_base, key_pair, key_force, key_shuffle = jax.random.split(jax.random.fold_in(key, 11), 5)
    per_peer = EXP_DEV // N_SEQ
    arrivals = jax.vmap(lambda single: jax.random.permutation(single, EXP_DEV))(jax.random.split(key_perm, N_SEQ))
    slot_grid = arrivals.reshape(N_SEQ, N_SEQ, per_peer) + (jnp.arange(N_SEQ, dtype=jnp.int32) * EXP_DEV)[:, None, None]
    order_ids = jnp.transpose(slot_grid, (1, 0, 2)).reshape(-1).astype(jnp.int32)
    base_owner = jax.random.randint(key_base, (N_SEQ,), 0, N_SEQ)
    paired = jax.random.randint(key_pair, (N_SEQ,), 0, 2)
    forced = jax.random.randint(key_force, (), 0, N_SEQ)
    paired = jnp.where(jnp.arange(N_SEQ) == forced, 1, paired)
    shuffled = jax.vmap(lambda single: jax.random.permutation(single, EXP_DEV))(jax.random.split(key_shuffle, N_SEQ))
    offsets = jnp.where(paired[:, None] == 1, shuffled // CAP, shuffled)
    owner_by_slot = ((base_owner[:, None] + offsets) % N_SEQ).reshape(-1).astype(jnp.int32)
    owners = jnp.zeros((GROUP_EXPANSIONS,), jnp.int32).at[order_ids].set(owner_by_slot)
    return (order_ids, owners)


def draw_order(key, part):
    return owner_plan(key)[0]


def draw_parent_owner(key, part):
    return owner_plan(key)[1]


def draw_token_count(key, part):
    key_blocks, key_top, key_low = jax.random.split(jax.random.fold_in(key, 23), 3)
    top_blocks = TOKEN_SLOTS // SPAN
    blocks = jax.random.randint(key_blocks, (GROUP_EXPANSIONS,), 1, top_blocks + 1)
    longest = jax.random.randint(key_top, (), 0, GROUP_EXPANSIONS)
    shortest = (longest + 1 + jax.random.randint(key_low, (), 0, GROUP_EXPANSIONS - 1)) % GROUP_EXPANSIONS
    positions = jnp.arange(GROUP_EXPANSIONS)
    blocks = jnp.where(positions == longest, top_blocks, blocks)
    blocks = jnp.where(positions == shortest, 1, blocks)
    return (blocks * SPAN).astype(jnp.int32)


def draw_log_decay(key, part):
    every_key_row = jax.random.split(jax.random.fold_in(key, 37), 7)
    fast_share = 0.5
    fast_heads = jax.random.uniform(every_key_row[0], (KEY_HEAD_COUNT, 2)) < fast_share
    fast_rate = jnp.exp(jax.random.uniform(every_key_row[1], (KEY_HEAD_COUNT, 2), jnp.float32, jnp.log(1.0 / 50.0), jnp.log(1.0 / 30.0)))
    slow_rate = jnp.exp(jax.random.uniform(every_key_row[2], (KEY_HEAD_COUNT, 2), jnp.float32, jnp.log(3e-05), jnp.log(0.0006)))
    per_head_rate = jnp.where(fast_heads, fast_rate, slow_rate)
    growth_multiplier = jnp.exp(jax.random.uniform(every_key_row[3], (GROUP_EXPANSIONS, 1, 1, 1), jnp.float32, jnp.log(0.5), jnp.log(2.0)))
    jaggedness = jax.random.uniform(every_key_row[4], (GROUP_EXPANSIONS, TOKEN_SLOTS, KEY_HEAD_COUNT, 2), jnp.float32, 0.5, 1.5)
    flurries = jax.random.uniform(every_key_row[5], (GROUP_EXPANSIONS, TOKEN_SLOTS, KEY_HEAD_COUNT, 2)) < 2.0 / TOKEN_SLOTS
    flurry_depth = jnp.log(jax.random.uniform(every_key_row[6], (GROUP_EXPANSIONS, TOKEN_SLOTS, KEY_HEAD_COUNT, 2), jnp.float32, 0.5, 0.8))
    return (-(per_head_rate * growth_multiplier * jaggedness) + jnp.where(flurries, flurry_depth, 0.0)).astype(jnp.bfloat16)


def touch_ends(drawn, key, smallest, high):
    shape = drawn.shape
    spot = [jax.random.randint(jax.random.fold_in(key, axis), (), 0, shape[axis]) for axis in range(len(shape))]
    drawn = drawn.at[tuple(spot)].set(smallest)
    longest = shape.index(max(shape))
    spot[longest] = (spot[longest] + 1) % shape[longest]
    return drawn.at[tuple(spot)].set(high)


def levels(rng, extent, cuts, smallest, high):
    gain, own = 1.0, jax.random.fold_in(rng, 6)
    for axis_at, parts in cuts:
        heights = jnp.exp(jax.random.uniform(jax.random.fold_in(own, axis_at), (parts,), jnp.float32, smallest / len(cuts), high / len(cuts)))
        gain = gain * jnp.repeat(heights, extent[axis_at] // parts).reshape([-1 if axis == axis_at else 1 for axis in range(len(extent))])
    return gain


def scatter_about(own_key, shape, width, bound, cuts=(), kind=jnp.bfloat16):
    values = width * jax.random.normal(own_key, shape, jnp.float32)
    if cuts:
        values = values * levels(own_key, shape, cuts, -0.22, 0.18)
    return jnp.clip(values, -bound, bound).astype(kind)


def setup_inputs(seed: int = 0, part: int = 0) -> dict:
    arg_keys = jax.random.split(jax.random.key(seed), 12)
    part_keys = jax.random.split(jax.random.fold_in(arg_keys[11], part), 12)
    queries = scatter_about(part_keys[0], (GROUP_EXPANSIONS, TOKEN_SLOTS, KEY_HEAD_COUNT, DK), 1.0, 6.0, ((0, 4), (2, 4)))
    keys = scatter_about(part_keys[1], (GROUP_EXPANSIONS, TOKEN_SLOTS, KEY_HEAD_COUNT, DK), 1.0, 6.0, ((0, 4), (2, 4)))
    values = scatter_about(part_keys[2], (GROUP_EXPANSIONS, TOKEN_SLOTS, KEY_HEAD_COUNT, 2, DV), 1.0, 6.0, ((0, 4), (2, 4)))
    log_decay = draw_log_decay(jax.random.fold_in(jax.random.fold_in(arg_keys[11], part), 71), part)
    write_rate = jnp.clip(0.049804688 + 0.89941406 * jax.random.uniform(part_keys[4], (GROUP_EXPANSIONS, TOKEN_SLOTS, KEY_HEAD_COUNT, 2), jnp.float32) ** levels(part_keys[4], (GROUP_EXPANSIONS, TOKEN_SLOTS, KEY_HEAD_COUNT, 2), ((0, 4), (2, 4)), -0.2, 0.2), 0.049804688, 0.94921875).astype(jnp.bfloat16)
    norm_gain = jnp.clip(1.0 + 0.15 * jax.random.normal(arg_keys[5], (DV,), jnp.float32), 0.25, 1.75).astype(jnp.bfloat16)
    parent_cache = scatter_about(part_keys[6], (PARENTS, KEY_HEAD_COUNT, 2, DK, DV), 0.5, 3.0, ((0, 4), (1, 4)), jnp.float32)
    order = draw_order(jax.random.fold_in(jax.random.fold_in(arg_keys[11], part), 71), part)
    parent_owner = draw_parent_owner(jax.random.fold_in(jax.random.fold_in(arg_keys[11], part), 71), part)
    parent_slot = touch_ends(jax.random.randint(part_keys[9], (GROUP_EXPANSIONS,), 0, PAR_DEV), jax.random.fold_in(part_keys[9], 1), 0, PAR_DEV - 1).astype(jnp.int32)
    token_count = draw_token_count(jax.random.fold_in(jax.random.fold_in(arg_keys[11], part), 71), part)
    return {"queries": queries, "keys": keys, "values": values, "log_decay": log_decay, "write_rate": write_rate, "norm_gain": norm_gain, "parent_cache": parent_cache, "order": order, "parent_owner": parent_owner, "parent_slot": parent_slot, "token_count": token_count}


exact_mode = lax.Precision.HIGHEST
norm_epsilon = 1e-06

def inverse_unit(lower_part):
    block_len = lower_part.shape[-1]
    identity = jnp.eye(block_len, dtype=jnp.float32)
    result = identity - lower_part
    powered = lower_part
    for repeat_no in range(block_len.bit_length() - 2):
        powered = jnp.einsum('...ij,...jk->...ik', powered, powered, precision=exact_mode)
        result = result + jnp.einsum('...ij,...jk->...ik', result, powered, precision=exact_mode)
    return result

def arrange(queries, keys, values, log_decay, write_rate, token_count, block_len):
    expansions, length, key_heads, key_dim = queries.shape
    value_dim = values.shape[-1]
    block_count = length // block_len
    head_rows = expansions * key_heads * 2
    positions = lax.broadcasted_iota(jnp.int32, (expansions, length), 1)
    live_mask = positions < token_count[:, None]
    keys_unit = keys.astype(jnp.float32)
    keys_unit = keys_unit / jnp.sqrt(lax.optimization_barrier(jnp.sum(keys_unit * keys_unit, axis=-1, keepdims=True)) + norm_epsilon)

    def spread_heads(tensor):
        turned = jnp.transpose(tensor, (0, 2, 1, 3))[:, :, None]
        widened = jnp.broadcast_to(turned, (expansions, key_heads, 2, length, key_dim))
        return widened.reshape(head_rows, block_count, block_len, key_dim)
    query_rows = spread_heads(queries.astype(jnp.float32))
    key_rows = spread_heads(keys_unit)
    value_rows = jnp.transpose(values.astype(jnp.float32), (0, 2, 3, 1, 4)).reshape(head_rows, block_count, block_len, value_dim)
    live_wide = live_mask[:, :, None, None]
    decay_rows = jnp.transpose(jnp.where(live_wide, log_decay.astype(jnp.float32), 0.0), (0, 2, 3, 1)).reshape(head_rows, block_count, block_len)
    rate_rows = jnp.transpose(jnp.where(live_wide, write_rate.astype(jnp.float32), 0.0), (0, 2, 3, 1)).reshape(head_rows, block_count, block_len)
    live_rows = jnp.broadcast_to(live_mask[:, None, None, :], (expansions, key_heads, 2, length)).reshape(head_rows, length)
    return (query_rows, key_rows, value_rows, decay_rows, rate_rows, live_rows)

def within_spans(query_rows, key_rows, value_rows, decay_rows, rate_rows):
    block_len = decay_rows.shape[-1]
    cumulative = jnp.cumsum(decay_rows, axis=-1)
    spread_log = cumulative[..., :, None] - cumulative[..., None, :]
    row_ids = lax.broadcasted_iota(jnp.int32, (block_len, block_len), 0)
    col_ids = lax.broadcasted_iota(jnp.int32, (block_len, block_len), 1)
    inclusive = row_ids >= col_ids
    strict = row_ids > col_ids
    decay_pair = jnp.where(inclusive, jnp.exp(jnp.where(inclusive, spread_log, 0.0)), 0.0)
    key_key = jnp.einsum('bncd,bnjd->bncj', key_rows, key_rows, precision=exact_mode)
    lower_part = jnp.where(strict, rate_rows[..., :, None] * key_key * decay_pair, 0.0)
    inverse = inverse_unit(lower_part)
    scaled_keys = key_rows * (rate_rows * jnp.exp(cumulative))[..., None]
    scaled_values = value_rows * rate_rows[..., None]
    weights_w = jnp.einsum('bncj,bnjd->bncd', inverse, scaled_keys, precision=exact_mode)
    updates_u = jnp.einsum('bncj,bnjd->bncd', inverse, scaled_values, precision=exact_mode)
    query_key = jnp.einsum('bncd,bnjd->bncj', query_rows, key_rows, precision=exact_mode)
    local_mix = query_key * decay_pair
    decayed_queries = query_rows * jnp.exp(cumulative)[..., None]
    decayed_keys = key_rows * jnp.exp(cumulative[..., -1:] - cumulative)[..., None]
    span_decay = jnp.exp(cumulative[..., -1])
    return (weights_w, updates_u, decayed_queries, decayed_keys, local_mix, span_decay)

def span_step(carried, pieces):
    weights_w, updates_u, decayed_queries, decayed_keys, local_mix, span_decay = pieces
    corrected = updates_u - jnp.einsum('bcd,bde->bce', weights_w, carried, precision=exact_mode)
    output = jnp.einsum('bcd,bde->bce', decayed_queries, carried, precision=exact_mode)
    output = output + jnp.einsum('bcj,bje->bce', local_mix, corrected, precision=exact_mode)
    carried = span_decay[:, None, None] * carried + jnp.einsum('bcd,bce->bde', decayed_keys, corrected, precision=exact_mode)
    return (carried, output)

def finish(outputs, norm_gain, live_rows):
    mean_square = lax.optimization_barrier(jnp.mean(outputs * outputs, axis=-1, keepdims=True))
    normed = outputs * lax.rsqrt(mean_square + norm_epsilon) * norm_gain.astype(jnp.float32)
    return jnp.where(live_rows[..., None], normed, 0.0).astype(jnp.bfloat16)

def restore(mixed_rows, expansions, key_heads):
    head_rows, length, value_dim = mixed_rows.shape
    return jnp.transpose(mixed_rows.reshape(expansions, key_heads, 2, length, value_dim), (0, 3, 1, 2, 4))

def reference(queries, keys, values, log_decay, write_rate, norm_gain, parent_cache, order, parent_owner, parent_slot, token_count):
    key_heads = queries.shape[2]
    parents = (parent_owner * PAR_DEV + parent_slot).astype(jnp.int32)

    def one_expansion(number):

        def pick_rows(tensor):
            return lax.dynamic_slice_in_dim(tensor, number, 1, 0)
        arranged = arrange(pick_rows(queries), pick_rows(keys), pick_rows(values), pick_rows(log_decay), pick_rows(write_rate), pick_rows(token_count), SPAN)
        query_rows, key_rows, value_rows, decay_rows, rate_rows, live_rows = arranged
        pieces = within_spans(query_rows, key_rows, value_rows, decay_rows, rate_rows)
        stacked = tuple((jnp.moveaxis(tensor, 1, 0) for tensor in pieces))
        initial = lax.dynamic_index_in_dim(parent_cache, parents[number], 0, keepdims=False)
        initial = initial.reshape(key_heads * 2, initial.shape[-2], initial.shape[-1])
        final_states, outputs = lax.scan(span_step, initial, stacked)
        outputs = jnp.moveaxis(outputs, 0, 1)
        outputs = outputs.reshape(key_heads * 2, -1, outputs.shape[-1])
        mixed_one = restore(finish(outputs, norm_gain, live_rows), 1, key_heads)
        return (mixed_one[0], final_states.reshape(key_heads, 2, final_states.shape[-2], final_states.shape[-1]))
    numbers = jnp.arange(queries.shape[0], dtype=jnp.int32)
    mixed_all, finals = lax.map(one_expansion, numbers)
    return (mixed_all, jnp.take(finals, order, axis=0))
```

```python
import functools

import jax
import jax.numpy as jnp
from jax import lax
from jax.experimental import pallas as pl
from jax.experimental.pallas import tpu as pltpu
from jax.sharding import PartitionSpec as P

norm_epsilon = 1e-06
BASE = 16
F32 = jnp.float32
BF16 = jnp.bfloat16
VMEM_BYTES = 56 * 1024 * 1024


def split(x):
    high = x.astype(BF16)
    low = (x - high.astype(F32)).astype(BF16)
    return high, low


def dot(a, b):
    return jnp.dot(a, b, preferred_element_type=F32)


def dot_nt(a, b):
    return lax.dot_general(a, b, (((1,), (1,)), ((), ())), preferred_element_type=F32)


def dot_tn(a, b):
    return lax.dot_general(a, b, (((0,), (0,)), ((), ())), preferred_element_type=F32)


def dot3(a, b):
    a_high, a_low = split(a)
    b_high, b_low = split(b)
    right = jnp.concatenate([b_high, b_low], axis=1)
    both = dot(jnp.concatenate([a_high, a_low], axis=1), jnp.concatenate([right, right], axis=0))
    width = b.shape[1]
    return both[:, :width] + both[:, width:]


CODE_BITS = 15
CODE_ROWS = 8
MESH = pl.DeviceIdType.MESH


def padded_rows(count):
    return -(-count // CODE_ROWS) * CODE_ROWS


def code_state(state):
    largest = jnp.maximum(jnp.max(jnp.abs(state), axis=0, keepdims=True), 1e-30)
    power = jnp.ceil(jnp.log2(largest)) - CODE_BITS
    limit = float(2**CODE_BITS - 1)
    code = jnp.clip(jnp.round(state * jnp.exp2(-power)), -limit, limit)
    return code.astype(jnp.int32), power.astype(jnp.int32)


def code_pair(states):
    (low, low_power), (high, high_power) = [code_state(state) for state in states]
    return (high << 16) | (low & 0xFFFF), [low_power, high_power]


def stack_powers(powers):
    spare = [jnp.zeros_like(powers[0])] * (padded_rows(len(powers)) - len(powers))
    return jnp.concatenate(powers + spare, axis=0)


def decode_pair(word, scales):
    codes = [(word << 16) >> 16, word >> 16]
    return [code.astype(F32) * scale for code, scale in zip(codes, scales)]


def encode_chunk(parents, blocks, scales, chunk, me):
    count = parents.shape[1]
    powers = []
    for i in range(count):
        word, pair_powers = code_pair([parents[chunk, i, 0], parents[chunk, i, 1]])
        blocks[chunk, me, i] = word
        powers += pair_powers
    scales[chunk, me] = stack_powers(powers)


def decode_chunk(chunk, source, blocks, scales, states):
    count, _, width = blocks.shape[2:]
    factors = jnp.exp2(scales[chunk, source].astype(F32))
    for i in range(count):
        pair = decode_pair(
            blocks[chunk, source, i], [factors[2 * i + r:2 * i + r + 1, :] for r in range(2)]
        )
        for r in range(2):
            states[source, i, :, r * width:(r + 1) * width] = pair[r]


def unpack_expansion(e, live, q_raw, k_raw, v_raw, g_ref, b_ref, q_rows, k_rows, v_rows, q_heads,
                     k_heads, v_heads, gates):
    key_heads, _, length, _ = q_heads.shape
    value_heads = 2 * key_heads
    q_rows[...] = q_raw[e].astype(F32)
    k_rows[...] = k_raw[e].astype(F32)
    v_rows[...] = v_raw[e].astype(F32)
    alive = lax.broadcasted_iota(jnp.int32, (value_heads, length), 1) < live
    g = jnp.where(alive, g_ref[e].astype(F32), 0.0)
    b = jnp.where(alive, b_ref[e].astype(F32), 0.0)
    spare = jnp.zeros((4, length), F32)
    for m in range(key_heads):
        q_heads[m, e] = q_rows[pl.ds(m, length, stride=key_heads), :].astype(BF16)
        k_heads[m, e] = k_rows[pl.ds(m, length, stride=key_heads), :].astype(BF16)
        for r in range(2):
            h = 2 * m + r
            v_heads[m, e, r] = v_rows[pl.ds(h, length, stride=value_heads), :].astype(BF16)
        gates[m, e] = jnp.concatenate([g[2 * m:2 * m + 2], b[2 * m:2 * m + 2], spare], axis=0)


def prepare_group(group, chunk, ids, q_heads, k_heads, gates, t_ref, m_ref, aux_ref, a_rows):
    length = q_heads.shape[2]
    value_heads = 2 * len(ids)
    row = lax.broadcasted_iota(jnp.int32, (length, length), 0)
    col = lax.broadcasted_iota(jnp.int32, (length, length), 1)
    inclusive = row >= col
    strict = row > col
    diagonal = row == col
    ones_low = inclusive.astype(F32).astype(BF16)
    ones_up = (row <= col).astype(F32).astype(BF16)
    eye = diagonal.astype(F32).astype(BF16)
    picked = [gates[chunk, e] for e in ids]
    g_narrow = jnp.concatenate([gate[0:2] for gate in picked], axis=0).astype(BF16)
    b_narrow = jnp.concatenate([gate[2:4] for gate in picked], axis=0).astype(BF16)
    g_col = dot_nt(ones_low, g_narrow)
    g_row = dot(g_narrow, ones_up)
    b = dot_nt(eye, b_narrow)
    lane = lax.broadcasted_iota(jnp.int32, (BASE, length), 1)
    sub = lax.broadcasted_iota(jnp.int32, (BASE, length), 0)
    parts = length // BASE
    unit_cols = []
    compact = []
    for m, e in enumerate(ids):
        q = q_heads[chunk, e]
        k = k_heads[chunk, e]
        both = dot_nt(jnp.concatenate([k, q], axis=0), k)
        kk = both[:length]
        qk = both[length:]
        squares = jnp.where(diagonal, kk, 0.0)
        n_row = lax.rsqrt(jnp.sum(squares, axis=0, keepdims=True) + norm_epsilon)
        n_col = lax.rsqrt(jnp.sum(squares, axis=1, keepdims=True) + norm_epsilon)
        unit_cols += [n_col, n_col]
        kk = kk * n_row * n_col
        qk = qk * n_row
        for r in range(2):
            h = 2 * m + r
            decay = jnp.exp(jnp.where(inclusive, g_col[:, h:h + 1] - g_row[h:h + 1, :], 0.0))
            m_ref[group, h] = jnp.where(inclusive, qk * decay, 0.0)
            a = jnp.where(strict, kk * decay * b[:, h:h + 1], 0.0)
            a_rows[h] = a
            piece = jnp.zeros((BASE, length), F32)
            for p in range(parts):
                piece = jnp.where(lane // BASE == p, a[p * BASE:(p + 1) * BASE], piece)
            compact.append(piece)
    inverses = [(lane % BASE == sub).astype(F32) for _ in range(value_heads)]
    for j in range(BASE - 1):
        index = (lane // BASE) * BASE + j
        for h in range(value_heads):
            factor = jnp.take_along_axis(compact[h], index, axis=1)
            inverses[h] = inverses[h] - factor * inverses[h][j:j + 1, :]
    block_masks = [lane // BASE == p for p in range(parts)]
    levels = []
    size = BASE
    while size < length:
        levels.append((size, range(size, length, 2 * size)))
        size *= 2
    heads = range(value_heads)
    for h in heads:
        blocks = [jnp.where(block_masks[p], inverses[h], 0.0) for p in range(parts)]
        t_ref[group, h] = jnp.concatenate(blocks, axis=0)
    for size, starts in levels:
        columns = lax.broadcasted_iota(jnp.int32, (size, length), 1) // size
        empty = jnp.zeros((size, length), F32)
        steps = []
        for h in heads:
            lower = [
                jnp.where(columns == start // size - 1, a_rows[h, start:start + size, :], 0.0)
                for start in starts
            ]
            steps.append(dot3(jnp.concatenate(lower, axis=0), t_ref[group, h]))
        for h in heads:
            spread = []
            for n in range(len(starts)):
                spread += [empty, steps[h][n * size:(n + 1) * size]]
            odd = jnp.concatenate(
                [t_ref[group, h, start:start + size, :] for start in starts], axis=0
            )
            odd = odd - dot3(odd, jnp.concatenate(spread, axis=0))
            for n, start in enumerate(starts):
                t_ref[group, h, start:start + size, :] = odd[n * size:(n + 1) * size]
    units = jnp.concatenate(unit_cols, axis=1)
    growth = jnp.exp(g_col)
    rest = jnp.exp(g_col[length - 1:length, :] - g_col) * units
    aux_ref[group] = jnp.concatenate([growth, b, b * growth * units, rest], axis=1)


def advance_group(group, chunk, ids, lives, owners, slots, q_heads, k_heads, v_heads, t_ref, m_ref,
                  aux_ref, gain, states, stage, o_rows):
    length, key_dim = q_heads.shape[2:]
    width = v_heads.shape[-1]
    value_heads = 2 * len(ids)
    all_heads = 2 * q_heads.shape[0]
    aux = aux_ref[group]
    columns = lambda n, h: aux[:, n * value_heads + h:n * value_heads + h + 1]
    half = lambda pair, r: pair[:, r * width:(r + 1) * width]
    token = lax.broadcasted_iota(jnp.int32, (length, width), 0)
    keys, applied = [], []
    for m, e in enumerate(ids):
        q = q_heads[chunk, e]
        k = k_heads[chunk, e]
        s_high, s_low = split(states[owners[m], slots[m]])
        kq = jnp.concatenate([k, q], axis=0)
        keys.append(k)
        applied.append(
            dot(jnp.concatenate([kq, kq], axis=1), jnp.concatenate([s_high, s_low], axis=0))
        )
    fixed = []
    for h in range(value_heads):
        v = v_heads[chunk, ids[h // 2], h % 2].astype(F32)
        right = columns(1, h) * v - columns(2, h) * half(applied[h // 2][:length], h % 2)
        fixed.append(dot3(t_ref[group, h], right))
    powers = []
    for m, e in enumerate(ids):
        k = keys[m]
        update = jnp.concatenate(
            [columns(3, 2 * m + r) * fixed[2 * m + r] for r in range(2)], axis=1
        )
        u_high, u_low = split(update)
        added = dot_tn(jnp.concatenate([k, k], axis=0), jnp.concatenate([u_high, u_low], axis=0))
        state = states[owners[m], slots[m]]
        later = []
        for r in range(2):
            last = aux[length - 1:length, 2 * m + r:2 * m + r + 1]
            later.append(last * half(state, r) + half(added, r))
        word, pair_powers = code_pair(later)
        stage[chunk, group, m * key_dim:(m + 1) * key_dim, :] = word
        powers += pair_powers
    stage[chunk, group, len(ids) * key_dim:, :] = stack_powers(powers)
    for h in range(value_heads):
        out = columns(0, h) * half(applied[h // 2][length:], h % 2)
        out = out + dot3(m_ref[group, h], fixed[h])
        mean_square = jnp.mean(out * out, axis=1, keepdims=True)
        normed = out * lax.rsqrt(mean_square + norm_epsilon) * gain
        rows = pl.ds(2 * chunk + h % 2, length, stride=all_heads)
        o_rows[group * len(ids) + h // 2, rows, :] = jnp.where(token < lives[h // 2], normed, 0.0)


def exchange_kernel(order_ref, owner_ref, slot_ref, count_ref, gain_ref, g_ref, b_ref, q_any, k_any,
                    v_any, parents_any, mixed_any, codes_any, parents, q_raw, k_raw, v_raw, q_rows,
                    k_rows, v_rows, q_heads, k_heads, v_heads, gates, t_ref, m_ref, aux_ref, a_rows,
                    blocks, scales, states, stage, o_rows, mixed, parent_sem, raw_sem, mixed_sem, line_send,
                    line_recv, final_send, final_recv):
    ring = lax.axis_size("seq")
    me = lax.axis_index("seq")
    chunks, expansions = q_heads.shape[:2]
    groups = ring
    per_peer = expansions // ring

    def parent_copy(c):
        return pltpu.make_async_copy(
            parents_any.at[:, 2 * c:2 * c + 2], parents.at[c], parent_sem.at[c]
        )

    def raw_copies(e):
        pairs = ((q_any, q_raw), (k_any, k_raw), (v_any, v_raw))
        return [
            pltpu.make_async_copy(a.at[e], b.at[e], raw_sem.at[e, n])
            for n, (a, b) in enumerate(pairs)
        ]

    def line_copies(c, way, hop, source, peer):
        return [
            pltpu.make_async_remote_copy(
                src_ref=held.at[c, source],
                dst_ref=held.at[c, source],
                send_sem=line_send.at[c, way, hop, n],
                recv_sem=line_recv.at[c, way, hop, n],
                device_id={"seq": peer},
                device_id_type=MESH,
            )
            for n, held in enumerate((scales, blocks))
        ]

    def line_start(c):
        @pl.when(me < ring - 1)
        def _():
            for copy in line_copies(c, 0, 0, me, me + 1):
                copy.start()

        @pl.when(me > 0)
        def _():
            for copy in line_copies(c, 1, 0, me, me - 1):
                copy.start()

    def line_hop(c, hop):
        for way, step in ((0, 1), (1, -1)):
            source = me - step * hop
            inside = (source >= 0) & (source <= ring - 1)
            onward = inside & (me + step >= 0) & (me + step <= ring - 1)

            @pl.when(inside)
            def _():
                for copy in line_copies(c, way, hop - 1, source, me - step):
                    copy.wait_recv()

            @pl.when(onward)
            def _():
                for copy in line_copies(c, way, hop, source, me + step):
                    copy.start()

    def line_drain(c, hop):
        for way, step in ((0, 1), (1, -1)):
            source = me - step * hop
            inside = (source >= 0) & (source <= ring - 1)
            onward = inside & (me + step >= 0) & (me + step <= ring - 1)

            @pl.when(onward)
            def _():
                for copy in line_copies(c, way, hop, source, me + step):
                    copy.wait_send()

    def final_copy(c, i, source, peer):
        return pltpu.make_async_remote_copy(
            src_ref=stage.at[c, i],
            dst_ref=codes_any.at[c, source],
            send_sem=final_send.at[c, i],
            recv_sem=final_recv.at[c, i],
            device_id={"seq": peer},
            device_id_type=MESH,
        )

    def own_copy(c):
        return pltpu.make_async_copy(
            stage.at[c, groups - 1], codes_any.at[c, me], final_send.at[c, groups - 1]
        )

    def mixed_copy(j):
        return pltpu.make_async_copy(mixed.at[j], mixed_any.at[j], mixed_sem.at[j])

    def members(i):
        first = lax.rem(me + 1 + i, ring) * expansions + me * per_peer
        return [order_ref[first + a] for a in range(per_peer)]

    for c in range(chunks):
        parent_copy(c).start()

    @pl.loop(0, expansions)
    def _(e):
        for copy in raw_copies(e):
            copy.start()

    barrier = pltpu.get_barrier_semaphore()
    for i in range(1, ring):
        pl.semaphore_signal(
            barrier, inc=1, device_id={"seq": lax.rem(me + i, ring)}, device_id_type=MESH
        )
    parent_copy(0).wait()
    encode_chunk(parents, blocks, scales, 0, me)
    pl.semaphore_wait(barrier, ring - 1)
    line_start(0)
    for c in range(1, chunks):
        parent_copy(c).wait()
        encode_chunk(parents, blocks, scales, c, me)

    @pl.loop(0, expansions)
    def _(e):
        for copy in raw_copies(e):
            copy.wait()
        unpack_expansion(e, count_ref[me * expansions + e], q_raw, k_raw, v_raw, g_ref, b_ref,
                         q_rows, k_rows, v_rows, q_heads, k_heads, v_heads, gates)

    line_hop(0, 1)
    gain = gain_ref[...].astype(F32)

    @pl.loop(0, chunks)
    def _(c):
        def tick(t):
            @pl.when(c + 1 < chunks)
            def _():
                @pl.when(t == 0)
                def _():
                    line_start(c + 1)

                @pl.when((t > 0) & (t % 2 == 0) & (t // 2 < ring - 1))
                def _():
                    line_hop(c + 1, t // 2)

        @pl.loop(0, groups)
        def _(i):
            tick(i)

            @pl.when((c == 0) & (i > 0) & (i + 1 < ring - 1))
            def _():
                line_hop(0, i + 1)

            ids = [jnp.maximum(number - me * expansions, 0) for number in members(i)]
            prepare_group(i, c, ids, q_heads, k_heads, gates, t_ref, m_ref, aux_ref, a_rows)

        line_hop(c, ring - 1)

        @pl.loop(0, ring)
        def _(source):
            decode_chunk(c, source, blocks, scales, states)

        @pl.loop(0, groups)
        def _(i):
            tick(groups + i)
            numbers = members(i)
            ids = [jnp.maximum(number - me * expansions, 0) for number in numbers]
            lives = [count_ref[number] for number in numbers]
            owners = [owner_ref[number] for number in numbers]
            slots = [slot_ref[number] for number in numbers]
            advance_group(i, c, ids, lives, owners, slots, q_heads, k_heads, v_heads, t_ref, m_ref,
                          aux_ref, gain, states, stage, o_rows)

            @pl.when(i < groups - 1)
            def _():
                final_copy(c, i, me, lax.rem(me + 1 + i, ring)).start()

            @pl.when(i == groups - 1)
            def _():
                own_copy(c).start()

            @pl.when(c == chunks - 1)
            def _():
                for a in range(per_peer):
                    j = i * per_peer + a
                    mixed[j] = o_rows[j].astype(BF16)
                    mixed_copy(j).start()

    @pl.loop(0, expansions)
    def _(j):
        mixed_copy(j).wait()

    @pl.loop(0, chunks)
    def _(c):
        own_copy(c).wait()

        @pl.loop(0, ring - 1)
        def _(hop):
            line_drain(c, hop)

        @pl.loop(0, groups - 1)
        def _(i):
            source = lax.rem(me + 2 * ring - 1 - i, ring)
            copy = final_copy(c, i, source, lax.rem(me + 1 + i, ring))
            copy.wait_send()
            copy.wait_recv()


def exchange(order, owner, slot, count, gain, decay, rate, queries, keys, values, parents, ring):
    expansions, rows, key_dim = queries.shape
    cached, value_heads, _, width = parents.shape
    chunks = value_heads // 2
    length = rows // chunks
    per_peer = expansions // ring
    heads = 2 * per_peer
    final_rows = per_peer * key_dim + padded_rows(2 * per_peer)
    anywhere = pl.BlockSpec(memory_space=pl.ANY)
    whole = pl.BlockSpec(memory_space=pltpu.VMEM)
    scalars = pl.BlockSpec(memory_space=pltpu.SMEM)
    work = expansions * value_heads
    return pl.pallas_call(
        exchange_kernel,
        out_shape=(
            jax.ShapeDtypeStruct(values.shape, BF16),
            jax.ShapeDtypeStruct((chunks, ring, final_rows, width), jnp.int32),
        ),
        in_specs=[scalars] * 4 + [whole] * 3 + [anywhere] * 4,
        out_specs=(anywhere, anywhere),
        scratch_shapes=[
            pltpu.VMEM((chunks, cached, 2, key_dim, width), F32),
            pltpu.VMEM(queries.shape, BF16),
            pltpu.VMEM(keys.shape, BF16),
            pltpu.VMEM(values.shape, BF16),
            pltpu.VMEM((rows, key_dim), F32),
            pltpu.VMEM((rows, key_dim), F32),
            pltpu.VMEM((length * value_heads, width), F32),
            pltpu.VMEM((chunks, expansions, length, key_dim), BF16),
            pltpu.VMEM((chunks, expansions, length, key_dim), BF16),
            pltpu.VMEM((chunks, expansions, 2, length, width), BF16),
            pltpu.VMEM((chunks, expansions, 8, length), F32),
            pltpu.VMEM((ring, heads, length, length), F32),
            pltpu.VMEM((ring, heads, length, length), F32),
            pltpu.VMEM((ring, length, 4 * heads), F32),
            pltpu.VMEM((heads, length, length), F32),
            pltpu.VMEM((chunks, ring, cached, key_dim, width), jnp.int32),
            pltpu.VMEM((chunks, ring, padded_rows(2 * cached), width), jnp.int32),
            pltpu.VMEM((ring, cached, key_dim, 2 * width), F32),
            pltpu.VMEM((chunks, ring, final_rows, width), jnp.int32),
            pltpu.VMEM(values.shape, F32),
            pltpu.VMEM(values.shape, BF16),
            pltpu.SemaphoreType.DMA((chunks,)),
            pltpu.SemaphoreType.DMA((expansions, 3)),
            pltpu.SemaphoreType.DMA((expansions,)),
            pltpu.SemaphoreType.DMA((chunks, 2, ring - 1, 2)),
            pltpu.SemaphoreType.DMA((chunks, 2, ring - 1, 2)),
            pltpu.SemaphoreType.DMA((chunks, ring)),
            pltpu.SemaphoreType.DMA((chunks, ring)),
        ],
        compiler_params=pltpu.CompilerParams(
            vmem_limit_bytes=VMEM_BYTES, collective_id=0, has_side_effects=True
        ),
        cost_estimate=pl.CostEstimate(
            flops=work * 40 * length**3,
            bytes_accessed=work * length**2 * 16,
            transcendentals=work * length**2,
        ),
        name="exchange",
    )(order, owner, slot, count, gain, decay, rate, queries, keys, values, parents)


def finish_kernel(ring, order_ref, codes_ref, slots_any, state_ref, mixed_any, held, in_sem,
                  out_sem):
    step = pl.program_id(0)
    me = lax.axis_index("seq")
    per_peer, value_heads, key_dim, _ = state_ref.shape
    expansions = ring * per_peer

    def arrive(j):
        return pltpu.make_async_copy(slots_any.at[j], held.at[j], in_sem.at[j])

    def leave(i, a):
        j = i * per_peer + a
        first = lax.rem(me + 1 + i, ring) * expansions + me * per_peer
        number = order_ref[first + a] - me * expansions
        return pltpu.make_async_copy(held.at[j], mixed_any.at[number], out_sem.at[j])

    @pl.when(step == 0)
    def _():
        for j in range(expansions):
            arrive(j).start()

    for c in range(value_heads // 2):
        scales = jnp.exp2(codes_ref[c, 0, per_peer * key_dim:, :].astype(F32))
        for a in range(per_peer):
            word = codes_ref[c, 0, a * key_dim:(a + 1) * key_dim, :]
            pair = [scales[2 * a + r:2 * a + r + 1, :] for r in range(2)]
            state_ref[a, 2 * c], state_ref[a, 2 * c + 1] = decode_pair(word, pair)

    for a in range(per_peer):
        arrive(step * per_peer + a).wait()
        leave(step, a).start()

    @pl.when(step == ring - 1)
    def _():
        for i in range(ring):
            for a in range(per_peer):
                leave(i, a).wait()


def finish(order, codes, slots, state_shape, ring):
    expansions, value_heads, key_dim, width = state_shape
    chunks, _, rows, _ = codes.shape
    per_peer = expansions // ring
    return pl.pallas_call(
        functools.partial(finish_kernel, ring),
        out_shape=(
            jax.ShapeDtypeStruct(state_shape, F32),
            jax.ShapeDtypeStruct(slots.shape, BF16),
        ),
        grid_spec=pltpu.PrefetchScalarGridSpec(
            num_scalar_prefetch=1,
            grid=(ring,),
            in_specs=[
                pl.BlockSpec((chunks, 1, rows, width), lambda i, order: (0, i, 0, 0)),
                pl.BlockSpec(memory_space=pl.ANY),
            ],
            out_specs=(
                pl.BlockSpec((per_peer, value_heads, key_dim, width), lambda i, order: (i, 0, 0, 0)),
                pl.BlockSpec(memory_space=pl.ANY),
            ),
            scratch_shapes=[
                pltpu.VMEM(slots.shape, BF16),
                pltpu.SemaphoreType.DMA((expansions,)),
                pltpu.SemaphoreType.DMA((expansions,)),
            ],
        ),
        compiler_params=pltpu.CompilerParams(vmem_limit_bytes=VMEM_BYTES),
        name="finish",
    )(order, codes, slots)


def shards(queries, keys, values, log_decay, write_rate, norm_gain, parent_cache, order,
           parent_owner, parent_slot, token_count):
    ring = lax.axis_size("seq")
    expansions, length, key_heads, key_dim = queries.shape
    value_heads = 2 * key_heads
    width = values.shape[-1]
    cached = parent_cache.shape[0]
    turned = lambda x: x.transpose(0, 2, 3, 1).reshape(expansions, value_heads, length)
    slots, codes = exchange(
        order,
        parent_owner,
        parent_slot,
        token_count,
        norm_gain.reshape(1, width),
        turned(log_decay),
        turned(write_rate),
        queries.reshape(expansions, length * key_heads, key_dim),
        keys.reshape(expansions, length * key_heads, key_dim),
        values.reshape(expansions, length * value_heads, width),
        parent_cache.reshape(cached, value_heads, key_dim, width),
        ring,
    )
    final, mixed = finish(order, codes, slots, (expansions, value_heads, key_dim, width), ring)
    return (
        mixed.reshape(values.shape),
        final.reshape((expansions,) + parent_cache.shape[1:]),
    )


def solution(mesh):
    heads = ("head", "sub")
    rows = ("groups", "seq")
    placed = (
        P(rows, None, heads, None),
        P(rows, None, heads, None),
        P(rows, None, heads, None, None),
        P(rows, None, heads, None),
        P(rows, None, heads, None),
        P(),
        P(rows, heads, None, None, None),
        P("groups"),
        P("groups"),
        P("groups"),
        P("groups"),
    )
    return jax.shard_map(
        shards,
        mesh=mesh,
        in_specs=placed,
        out_specs=(P(rows, None, heads, None, None), P(rows, heads, None, None, None)),
        check_vma=False,
    )
```

```python
import functools

import jax
import jax.numpy as jnp
from jax import lax
from jax.experimental import pallas as pl
from jax.experimental.pallas import tpu as pltpu
from jax.sharding import PartitionSpec as P

norm_epsilon = 1e-06
BASE = 16
F32 = jnp.float32
BF16 = jnp.bfloat16
VMEM_BYTES = 24 * 1024 * 1024
EXCHANGE_BYTES = 46 * 1024 * 1024


def split(x):
    high = x.astype(BF16)
    low = (x - high.astype(F32)).astype(BF16)
    return high, low


def dot(a, b):
    return jnp.dot(a, b, preferred_element_type=F32)


def dot_nt(a, b):
    return lax.dot_general(a, b, (((1,), (1,)), ((), ())), preferred_element_type=F32)


def dot_tn(a, b):
    return lax.dot_general(a, b, (((0,), (0,)), ((), ())), preferred_element_type=F32)


def dot3(a, b):
    a_high, a_low = split(a)
    b_high, b_low = split(b)
    right = jnp.concatenate([b_high, b_low], axis=1)
    both = dot(jnp.concatenate([a_high, a_low], axis=1), jnp.concatenate([right, right], axis=0))
    width = b.shape[1]
    return both[:, :width] + both[:, width:]


CODE_BITS = 15
CODE_ROWS = 8
MESH = pl.DeviceIdType.MESH


def padded_rows(count):
    return -(-count // CODE_ROWS) * CODE_ROWS


def code_state(state):
    largest = jnp.maximum(jnp.max(jnp.abs(state), axis=0, keepdims=True), 1e-30)
    power = jnp.ceil(jnp.log2(largest)) - CODE_BITS
    limit = float(2**CODE_BITS - 1)
    code = jnp.clip(jnp.round(state * jnp.exp2(-power)), -limit, limit)
    return code.astype(jnp.int32), power.astype(jnp.int32)


def code_pair(states):
    (low, low_power), (high, high_power) = [code_state(state) for state in states]
    return (high << 16) | (low & 0xFFFF), [low_power, high_power]


def stack_powers(powers):
    spare = [jnp.zeros_like(powers[0])] * (padded_rows(len(powers)) - len(powers))
    return jnp.concatenate(powers + spare, axis=0)


def decode_pair(word, scales):
    codes = [(word << 16) >> 16, word >> 16]
    return [code.astype(F32) * scale for code, scale in zip(codes, scales)]


def encode_chunk(parents, blocks, scales, chunk, me):
    count = parents.shape[1]
    powers = []
    for i in range(count):
        word, pair_powers = code_pair([parents[chunk, i, 0], parents[chunk, i, 1]])
        blocks[chunk, me, i] = word
        powers += pair_powers
    scales[chunk, me] = stack_powers(powers)


def decode_chunk(chunk, source, blocks, scales, states):
    count, _, width = blocks.shape[2:]
    factors = jnp.exp2(scales[chunk, source].astype(F32))
    for i in range(count):
        pair = decode_pair(
            blocks[chunk, source, i], [factors[2 * i + r:2 * i + r + 1, :] for r in range(2)]
        )
        for r in range(2):
            states[source, i, :, r * width:(r + 1) * width] = pair[r]


def unpack_expansion(e, live, q_raw, k_raw, v_raw, g_ref, b_ref, q_rows, k_rows, v_rows, q_heads,
                     k_heads, v_heads, gates):
    key_heads, _, length, _ = q_heads.shape
    value_heads = 2 * key_heads
    q_rows[...] = q_raw[e].astype(F32)
    k_rows[...] = k_raw[e].astype(F32)
    v_rows[...] = v_raw[e].astype(F32)
    alive = lax.broadcasted_iota(jnp.int32, (value_heads, length), 1) < live
    g = jnp.where(alive, g_ref[e].astype(F32), 0.0)
    b = jnp.where(alive, b_ref[e].astype(F32), 0.0)
    spare = jnp.zeros((4, length), F32)
    for m in range(key_heads):
        q_heads[m, e] = q_rows[pl.ds(m, length, stride=key_heads), :].astype(BF16)
        k_heads[m, e] = k_rows[pl.ds(m, length, stride=key_heads), :].astype(BF16)
        for r in range(2):
            h = 2 * m + r
            v_heads[m, e, r] = v_rows[pl.ds(h, length, stride=value_heads), :].astype(BF16)
        gates[m, e] = jnp.concatenate([g[2 * m:2 * m + 2], b[2 * m:2 * m + 2], spare], axis=0)


def prepare_group(group, chunk, ids, q_heads, k_heads, gates, t_ref, m_ref, aux_ref, a_rows):
    length = q_heads.shape[2]
    value_heads = 2 * len(ids)
    row = lax.broadcasted_iota(jnp.int32, (length, length), 0)
    col = lax.broadcasted_iota(jnp.int32, (length, length), 1)
    inclusive = row >= col
    strict = row > col
    diagonal = row == col
    ones_low = inclusive.astype(F32).astype(BF16)
    ones_up = (row <= col).astype(F32).astype(BF16)
    eye = diagonal.astype(F32).astype(BF16)
    picked = [gates[chunk, e] for e in ids]
    g_narrow = jnp.concatenate([gate[0:2] for gate in picked], axis=0).astype(BF16)
    b_narrow = jnp.concatenate([gate[2:4] for gate in picked], axis=0).astype(BF16)
    g_col = dot_nt(ones_low, g_narrow)
    g_row = dot(g_narrow, ones_up)
    b = dot_nt(eye, b_narrow)
    lane = lax.broadcasted_iota(jnp.int32, (BASE, length), 1)
    sub = lax.broadcasted_iota(jnp.int32, (BASE, length), 0)
    parts = length // BASE
    unit_cols = []
    compact = []
    for m, e in enumerate(ids):
        q = q_heads[chunk, e]
        k = k_heads[chunk, e]
        both = dot_nt(jnp.concatenate([k, q], axis=0), k)
        kk = both[:length]
        qk = both[length:]
        squares = jnp.where(diagonal, kk, 0.0)
        n_row = lax.rsqrt(jnp.sum(squares, axis=0, keepdims=True) + norm_epsilon)
        n_col = lax.rsqrt(jnp.sum(squares, axis=1, keepdims=True) + norm_epsilon)
        unit_cols += [n_col, n_col]
        kk = kk * n_row * n_col
        qk = qk * n_row
        for r in range(2):
            h = 2 * m + r
            decay = jnp.exp(jnp.where(inclusive, g_col[:, h:h + 1] - g_row[h:h + 1, :], 0.0))
            m_ref[group, h] = jnp.where(inclusive, qk * decay, 0.0)
            a = jnp.where(strict, kk * decay * b[:, h:h + 1], 0.0)
            a_rows[h] = a
            piece = jnp.zeros((BASE, length), F32)
            for p in range(parts):
                piece = jnp.where(lane // BASE == p, a[p * BASE:(p + 1) * BASE], piece)
            compact.append(piece)
    inverses = [(lane % BASE == sub).astype(F32) for _ in range(value_heads)]
    for j in range(BASE - 1):
        index = (lane // BASE) * BASE + j
        for h in range(value_heads):
            factor = jnp.take_along_axis(compact[h], index, axis=1)
            inverses[h] = inverses[h] - factor * inverses[h][j:j + 1, :]
    block_masks = [lane // BASE == p for p in range(parts)]
    levels = []
    size = BASE
    while size < length:
        levels.append((size, range(size, length, 2 * size)))
        size *= 2
    heads = range(value_heads)
    for h in heads:
        blocks = [jnp.where(block_masks[p], inverses[h], 0.0) for p in range(parts)]
        t_ref[group, h] = jnp.concatenate(blocks, axis=0)
    for size, starts in levels:
        columns = lax.broadcasted_iota(jnp.int32, (size, length), 1) // size
        empty = jnp.zeros((size, length), F32)
        steps = []
        for h in heads:
            lower = [
                jnp.where(columns == start // size - 1, a_rows[h, start:start + size, :], 0.0)
                for start in starts
            ]
            steps.append(dot3(jnp.concatenate(lower, axis=0), t_ref[group, h]))
        for h in heads:
            spread = []
            for n in range(len(starts)):
                spread += [empty, steps[h][n * size:(n + 1) * size]]
            odd = jnp.concatenate(
                [t_ref[group, h, start:start + size, :] for start in starts], axis=0
            )
            odd = odd - dot3(odd, jnp.concatenate(spread, axis=0))
            for n, start in enumerate(starts):
                t_ref[group, h, start:start + size, :] = odd[n * size:(n + 1) * size]
    units = jnp.concatenate(unit_cols, axis=1)
    growth = jnp.exp(g_col)
    rest = jnp.exp(g_col[length - 1:length, :] - g_col) * units
    aux_ref[group] = jnp.concatenate([growth, b, b * growth * units, rest], axis=1)


def advance_group(group, chunk, ids, lives, owners, slots, q_heads, k_heads, v_heads, t_ref, m_ref,
                  aux_ref, gain, states, stage, o_rows):
    length, key_dim = q_heads.shape[2:]
    width = v_heads.shape[-1]
    value_heads = 2 * len(ids)
    all_heads = 2 * q_heads.shape[0]
    aux = aux_ref[group]
    columns = lambda n, h: aux[:, n * value_heads + h:n * value_heads + h + 1]
    half = lambda pair, r: pair[:, r * width:(r + 1) * width]
    token = lax.broadcasted_iota(jnp.int32, (length, width), 0)
    keys, applied = [], []
    for m, e in enumerate(ids):
        q = q_heads[chunk, e]
        k = k_heads[chunk, e]
        s_high, s_low = split(states[owners[m], slots[m]])
        kq = jnp.concatenate([k, q], axis=0)
        keys.append(k)
        applied.append(
            dot(jnp.concatenate([kq, kq], axis=1), jnp.concatenate([s_high, s_low], axis=0))
        )
    fixed = []
    for h in range(value_heads):
        v = v_heads[chunk, ids[h // 2], h % 2].astype(F32)
        right = columns(1, h) * v - columns(2, h) * half(applied[h // 2][:length], h % 2)
        fixed.append(dot3(t_ref[group, h], right))
    powers = []
    for m, e in enumerate(ids):
        k = keys[m]
        update = jnp.concatenate(
            [columns(3, 2 * m + r) * fixed[2 * m + r] for r in range(2)], axis=1
        )
        u_high, u_low = split(update)
        added = dot_tn(jnp.concatenate([k, k], axis=0), jnp.concatenate([u_high, u_low], axis=0))
        state = states[owners[m], slots[m]]
        later = []
        for r in range(2):
            last = aux[length - 1:length, 2 * m + r:2 * m + r + 1]
            later.append(last * half(state, r) + half(added, r))
        word, pair_powers = code_pair(later)
        stage[chunk, group, m * key_dim:(m + 1) * key_dim, :] = word
        powers += pair_powers
    stage[chunk, group, len(ids) * key_dim:, :] = stack_powers(powers)
    for h in range(value_heads):
        out = columns(0, h) * half(applied[h // 2][length:], h % 2)
        out = out + dot3(m_ref[group, h], fixed[h])
        mean_square = jnp.mean(out * out, axis=1, keepdims=True)
        normed = out * lax.rsqrt(mean_square + norm_epsilon) * gain
        rows = pl.ds(2 * chunk + h % 2, length, stride=all_heads)
        o_rows[group * len(ids) + h // 2, rows, :] = jnp.where(token < lives[h // 2], normed, 0.0)


def exchange_kernel(order_ref, owner_ref, slot_ref, count_ref, gain_ref, g_ref, b_ref, q_any, k_any,
                    v_any, parents_any, mixed, codes, parents, q_raw, k_raw, v_raw, q_rows,
                    k_rows, v_rows, q_heads, k_heads, v_heads, gates, t_ref, m_ref, aux_ref, a_rows,
                    blocks, scales, states, stage, o_rows, parent_sem, raw_sem, line_send,
                    line_recv, final_send, final_recv):
    ring = lax.axis_size("seq")
    me = lax.axis_index("seq")
    chunks, expansions = q_heads.shape[:2]
    groups = ring
    per_peer = expansions // ring

    def parent_copy(c):
        return pltpu.make_async_copy(
            parents_any.at[:, 2 * c:2 * c + 2], parents.at[c], parent_sem.at[c]
        )

    def raw_copies(e):
        pairs = ((q_any, q_raw), (k_any, k_raw), (v_any, v_raw))
        return [
            pltpu.make_async_copy(a.at[e], b.at[e], raw_sem.at[e, n])
            for n, (a, b) in enumerate(pairs)
        ]

    def line_copies(c, way, hop, source, peer):
        return [
            pltpu.make_async_remote_copy(
                src_ref=held.at[c, source],
                dst_ref=held.at[c, source],
                send_sem=line_send.at[c, way, hop, n],
                recv_sem=line_recv.at[c, way, hop, n],
                device_id={"seq": peer},
                device_id_type=MESH,
            )
            for n, held in enumerate((scales, blocks))
        ]

    def line_start(c):
        @pl.when(me < ring - 1)
        def _():
            for copy in line_copies(c, 0, 0, me, me + 1):
                copy.start()

        @pl.when(me > 0)
        def _():
            for copy in line_copies(c, 1, 0, me, me - 1):
                copy.start()

    def line_hop(c, hop):
        for way, step in ((0, 1), (1, -1)):
            source = me - step * hop
            inside = (source >= 0) & (source <= ring - 1)
            onward = inside & (me + step >= 0) & (me + step <= ring - 1)

            @pl.when(inside)
            def _():
                for copy in line_copies(c, way, hop - 1, source, me - step):
                    copy.wait_recv()

            @pl.when(onward)
            def _():
                for copy in line_copies(c, way, hop, source, me + step):
                    copy.start()

    def line_drain(c, hop):
        for way, step in ((0, 1), (1, -1)):
            source = me - step * hop
            inside = (source >= 0) & (source <= ring - 1)
            onward = inside & (me + step >= 0) & (me + step <= ring - 1)

            @pl.when(onward)
            def _():
                for copy in line_copies(c, way, hop, source, me + step):
                    copy.wait_send()

    def final_copy(c, i, source, peer):
        return pltpu.make_async_remote_copy(
            src_ref=stage.at[c, i],
            dst_ref=codes.at[c, source],
            send_sem=final_send.at[c, i],
            recv_sem=final_recv.at[c, i],
            device_id={"seq": peer},
            device_id_type=MESH,
        )

    def own_copy(c):
        return pltpu.make_async_copy(
            stage.at[c, groups - 1], codes.at[c, me], final_send.at[c, groups - 1]
        )

    def members(i):
        first = lax.rem(me + 1 + i, ring) * expansions + me * per_peer
        return [order_ref[first + a] for a in range(per_peer)]

    for c in range(chunks):
        parent_copy(c).start()

    @pl.loop(0, expansions)
    def _(e):
        for copy in raw_copies(e):
            copy.start()

    barrier = pltpu.get_barrier_semaphore()
    for i in range(1, ring):
        pl.semaphore_signal(
            barrier, inc=1, device_id={"seq": lax.rem(me + i, ring)}, device_id_type=MESH
        )
    parent_copy(0).wait()
    encode_chunk(parents, blocks, scales, 0, me)
    pl.semaphore_wait(barrier, ring - 1)
    line_start(0)
    for c in range(1, chunks):
        parent_copy(c).wait()
        encode_chunk(parents, blocks, scales, c, me)

    @pl.loop(0, expansions)
    def _(e):
        for copy in raw_copies(e):
            copy.wait()
        unpack_expansion(e, count_ref[me * expansions + e], q_raw, k_raw, v_raw, g_ref, b_ref,
                         q_rows, k_rows, v_rows, q_heads, k_heads, v_heads, gates)

    line_hop(0, 1)
    gain = gain_ref[...].astype(F32)

    @pl.loop(0, chunks)
    def _(c):
        def tick(t):
            @pl.when(c + 1 < chunks)
            def _():
                @pl.when(t == 0)
                def _():
                    line_start(c + 1)

                @pl.when((t > 0) & (t % 2 == 0) & (t // 2 < ring - 1))
                def _():
                    line_hop(c + 1, t // 2)

        @pl.loop(0, groups)
        def _(i):
            tick(i)

            @pl.when((c == 0) & (i > 0) & (i + 1 < ring - 1))
            def _():
                line_hop(0, i + 1)

            ids = [jnp.maximum(number - me * expansions, 0) for number in members(i)]
            prepare_group(i, c, ids, q_heads, k_heads, gates, t_ref, m_ref, aux_ref, a_rows)

        line_hop(c, ring - 1)

        @pl.loop(0, ring)
        def _(source):
            decode_chunk(c, source, blocks, scales, states)

        @pl.loop(0, groups)
        def _(i):
            tick(groups + i)
            numbers = members(i)
            ids = [jnp.maximum(number - me * expansions, 0) for number in numbers]
            lives = [count_ref[number] for number in numbers]
            owners = [owner_ref[number] for number in numbers]
            slots = [slot_ref[number] for number in numbers]
            advance_group(i, c, ids, lives, owners, slots, q_heads, k_heads, v_heads, t_ref, m_ref,
                          aux_ref, gain, states, stage, o_rows)

            @pl.when(i < groups - 1)
            def _():
                final_copy(c, i, me, lax.rem(me + 1 + i, ring)).start()

            @pl.when(i == groups - 1)
            def _():
                own_copy(c).start()

            @pl.when(c == chunks - 1)
            def _():
                for a in range(per_peer):
                    j = i * per_peer + a
                    mixed[j] = o_rows[j].astype(BF16)

    @pl.loop(0, chunks)
    def _(c):
        own_copy(c).wait()

        @pl.loop(0, ring - 1)
        def _(hop):
            line_drain(c, hop)

        @pl.loop(0, groups - 1)
        def _(i):
            source = lax.rem(me + 2 * ring - 1 - i, ring)
            copy = final_copy(c, i, source, lax.rem(me + 1 + i, ring))
            copy.wait_send()
            copy.wait_recv()


def exchange(order, owner, slot, count, gain, decay, rate, queries, keys, values, parents, ring):
    expansions, rows, key_dim = queries.shape
    cached, value_heads, _, width = parents.shape
    chunks = value_heads // 2
    length = rows // chunks
    per_peer = expansions // ring
    heads = 2 * per_peer
    final_rows = per_peer * key_dim + padded_rows(2 * per_peer)
    anywhere = pl.BlockSpec(memory_space=pl.ANY)
    whole = pl.BlockSpec(memory_space=pltpu.VMEM)
    scalars = pl.BlockSpec(memory_space=pltpu.SMEM)
    work = expansions * value_heads
    return pl.pallas_call(
        exchange_kernel,
        out_shape=(
            pltpu.VMEM(values.shape, BF16),
            pltpu.VMEM((chunks, ring, final_rows, width), jnp.int32),
        ),
        in_specs=[scalars] * 4 + [whole] * 3 + [anywhere] * 4,
        out_specs=(whole, whole),
        scratch_shapes=[
            pltpu.VMEM((chunks, cached, 2, key_dim, width), F32),
            pltpu.VMEM(queries.shape, BF16),
            pltpu.VMEM(keys.shape, BF16),
            pltpu.VMEM(values.shape, BF16),
            pltpu.VMEM((rows, key_dim), F32),
            pltpu.VMEM((rows, key_dim), F32),
            pltpu.VMEM((length * value_heads, width), F32),
            pltpu.VMEM((chunks, expansions, length, key_dim), BF16),
            pltpu.VMEM((chunks, expansions, length, key_dim), BF16),
            pltpu.VMEM((chunks, expansions, 2, length, width), BF16),
            pltpu.VMEM((chunks, expansions, 8, length), F32),
            pltpu.VMEM((ring, heads, length, length), F32),
            pltpu.VMEM((ring, heads, length, length), F32),
            pltpu.VMEM((ring, length, 4 * heads), F32),
            pltpu.VMEM((heads, length, length), F32),
            pltpu.VMEM((chunks, ring, cached, key_dim, width), jnp.int32),
            pltpu.VMEM((chunks, ring, padded_rows(2 * cached), width), jnp.int32),
            pltpu.VMEM((ring, cached, key_dim, 2 * width), F32),
            pltpu.VMEM((chunks, ring, final_rows, width), jnp.int32),
            pltpu.VMEM(values.shape, F32),
            pltpu.SemaphoreType.DMA((chunks,)),
            pltpu.SemaphoreType.DMA((expansions, 3)),
            pltpu.SemaphoreType.DMA((chunks, 2, ring - 1, 2)),
            pltpu.SemaphoreType.DMA((chunks, 2, ring - 1, 2)),
            pltpu.SemaphoreType.DMA((chunks, ring)),
            pltpu.SemaphoreType.DMA((chunks, ring)),
        ],
        compiler_params=pltpu.CompilerParams(
            vmem_limit_bytes=EXCHANGE_BYTES, collective_id=0, has_side_effects=True
        ),
        cost_estimate=pl.CostEstimate(
            flops=work * 40 * length**3,
            bytes_accessed=work * length**2 * 16,
            transcendentals=work * length**2,
        ),
        name="exchange",
    )(order, owner, slot, count, gain, decay, rate, queries, keys, values, parents)


def finish_kernel(ring, order_ref, codes_ref, slots_ref, state_ref, mixed_any, sems):
    step = pl.program_id(0)
    me = lax.axis_index("seq")
    per_peer, value_heads, key_dim, _ = state_ref.shape
    expansions = ring * per_peer

    def leave(i, a):
        j = i * per_peer + a
        first = lax.rem(me + 1 + i, ring) * expansions + me * per_peer
        number = order_ref[first + a] - me * expansions
        return pltpu.make_async_copy(slots_ref.at[j], mixed_any.at[number], sems.at[j])

    for a in range(per_peer):
        leave(step, a).start()

    for c in range(value_heads // 2):
        scales = jnp.exp2(codes_ref[c, step, per_peer * key_dim:, :].astype(F32))
        for a in range(per_peer):
            word = codes_ref[c, step, a * key_dim:(a + 1) * key_dim, :]
            pair = [scales[2 * a + r:2 * a + r + 1, :] for r in range(2)]
            state_ref[a, 2 * c], state_ref[a, 2 * c + 1] = decode_pair(word, pair)

    @pl.when(step == ring - 1)
    def _():
        for i in range(ring):
            for a in range(per_peer):
                leave(i, a).wait()


def finish(order, codes, slots, state_shape, ring):
    expansions, value_heads, key_dim, width = state_shape
    per_peer = expansions // ring
    return pl.pallas_call(
        functools.partial(finish_kernel, ring),
        out_shape=(
            jax.ShapeDtypeStruct(state_shape, F32),
            jax.ShapeDtypeStruct(slots.shape, BF16),
        ),
        grid_spec=pltpu.PrefetchScalarGridSpec(
            num_scalar_prefetch=1,
            grid=(ring,),
            in_specs=[pl.BlockSpec(memory_space=pltpu.VMEM), pl.BlockSpec(memory_space=pltpu.VMEM)],
            out_specs=(
                pl.BlockSpec((per_peer, value_heads, key_dim, width), lambda i, order: (i, 0, 0, 0)),
                pl.BlockSpec(memory_space=pl.ANY),
            ),
            scratch_shapes=[pltpu.SemaphoreType.DMA((expansions,))],
        ),
        compiler_params=pltpu.CompilerParams(vmem_limit_bytes=VMEM_BYTES),
        name="finish",
    )(
        order,
        pltpu.with_memory_space_constraint(codes, pltpu.VMEM),
        pltpu.with_memory_space_constraint(slots, pltpu.VMEM),
    )


def shards(queries, keys, values, log_decay, write_rate, norm_gain, parent_cache, order,
           parent_owner, parent_slot, token_count):
    ring = lax.axis_size("seq")
    expansions, length, key_heads, key_dim = queries.shape
    value_heads = 2 * key_heads
    width = values.shape[-1]
    cached = parent_cache.shape[0]
    turned = lambda x: x.transpose(0, 2, 3, 1).reshape(expansions, value_heads, length)
    slots, codes = exchange(
        order,
        parent_owner,
        parent_slot,
        token_count,
        norm_gain.reshape(1, width),
        turned(log_decay),
        turned(write_rate),
        queries.reshape(expansions, length * key_heads, key_dim),
        keys.reshape(expansions, length * key_heads, key_dim),
        values.reshape(expansions, length * value_heads, width),
        parent_cache.reshape(cached, value_heads, key_dim, width),
        ring,
    )
    final, mixed = finish(order, codes, slots, (expansions, value_heads, key_dim, width), ring)
    return (
        mixed.reshape(values.shape),
        final.reshape((expansions,) + parent_cache.shape[1:]),
    )


def solution(mesh):
    heads = ("head", "sub")
    rows = ("groups", "seq")
    placed = (
        P(rows, None, heads, None),
        P(rows, None, heads, None),
        P(rows, None, heads, None, None),
        P(rows, None, heads, None),
        P(rows, None, heads, None),
        P(),
        P(rows, heads, None, None, None),
        P("groups"),
        P("groups"),
        P("groups"),
        P("groups"),
    )
    return jax.shard_map(
        shards,
        mesh=mesh,
        in_specs=placed,
        out_specs=(P(rows, None, heads, None, None), P(rows, heads, None, None, None)),
        check_vma=False,
    )
```

```python
import functools

import jax
import jax.numpy as jnp
from jax import lax
from jax.experimental import pallas as pl
from jax.experimental.pallas import tpu as pltpu
from jax.sharding import PartitionSpec as P

norm_epsilon = 1e-06
BASE = 16
F32 = jnp.float32
BF16 = jnp.bfloat16
VMEM_BYTES = 24 * 1024 * 1024
EXCHANGE_BYTES = 46 * 1024 * 1024


def split(x):
    high = x.astype(BF16)
    low = (x - high.astype(F32)).astype(BF16)
    return high, low


def dot(a, b):
    return jnp.dot(a, b, preferred_element_type=F32)


def dot_nt(a, b):
    return lax.dot_general(a, b, (((1,), (1,)), ((), ())), preferred_element_type=F32)


def dot_tn(a, b):
    return lax.dot_general(a, b, (((0,), (0,)), ((), ())), preferred_element_type=F32)


def dot3(a, b):
    a_high, a_low = split(a)
    b_high, b_low = split(b)
    right = jnp.concatenate([b_high, b_low], axis=1)
    both = dot(jnp.concatenate([a_high, a_low], axis=1), jnp.concatenate([right, right], axis=0))
    width = b.shape[1]
    return both[:, :width] + both[:, width:]


CODE_BITS = 15
CODE_ROWS = 8
MESH = pl.DeviceIdType.MESH


def turn(ring, i):
    far = lax.div(i + 1, 2)
    return ring // 2 + jnp.where(lax.rem(i, 2) == 1, -far, far)


def padded_rows(count):
    return -(-count // CODE_ROWS) * CODE_ROWS


def code_state(state):
    largest = jnp.maximum(jnp.max(jnp.abs(state), axis=0, keepdims=True), 1e-30)
    power = jnp.ceil(jnp.log2(largest)) - CODE_BITS
    limit = float(2**CODE_BITS - 1)
    code = jnp.clip(jnp.round(state * jnp.exp2(-power)), -limit, limit)
    return code.astype(jnp.int32), power.astype(jnp.int32)


def code_pair(states):
    (low, low_power), (high, high_power) = [code_state(state) for state in states]
    return (high << 16) | (low & 0xFFFF), [low_power, high_power]


def stack_powers(powers):
    spare = [jnp.zeros_like(powers[0])] * (padded_rows(len(powers)) - len(powers))
    return jnp.concatenate(powers + spare, axis=0)


def decode_pair(word, scales):
    codes = [(word << 16) >> 16, word >> 16]
    return [code.astype(F32) * scale for code, scale in zip(codes, scales)]


def encode_chunk(parents, blocks, scales, chunk, me):
    count = parents.shape[1]
    powers = []
    for i in range(count):
        word, pair_powers = code_pair([parents[chunk, i, 0], parents[chunk, i, 1]])
        blocks[chunk, me, i] = word
        powers += pair_powers
    scales[chunk, me] = stack_powers(powers)


def decode_chunk(chunk, source, blocks, scales, states):
    count, _, width = blocks.shape[2:]
    factors = jnp.exp2(scales[chunk, source].astype(F32))
    for i in range(count):
        pair = decode_pair(
            blocks[chunk, source, i], [factors[2 * i + r:2 * i + r + 1, :] for r in range(2)]
        )
        for r in range(2):
            states[source, i, :, r * width:(r + 1) * width] = pair[r]


def unpack_expansion(e, live, q_raw, k_raw, v_raw, g_ref, b_ref, q_rows, k_rows, v_rows, q_heads,
                     k_heads, v_heads, gates):
    key_heads, _, length, _ = q_heads.shape
    value_heads = 2 * key_heads
    q_rows[...] = q_raw[e].astype(F32)
    k_rows[...] = k_raw[e].astype(F32)
    v_rows[...] = v_raw[e].astype(F32)
    alive = lax.broadcasted_iota(jnp.int32, (value_heads, length), 1) < live
    g = jnp.where(alive, g_ref[e].astype(F32), 0.0)
    b = jnp.where(alive, b_ref[e].astype(F32), 0.0)
    spare = jnp.zeros((4, length), F32)
    for m in range(key_heads):
        q_heads[m, e] = q_rows[pl.ds(m, length, stride=key_heads), :].astype(BF16)
        k_heads[m, e] = k_rows[pl.ds(m, length, stride=key_heads), :].astype(BF16)
        for r in range(2):
            h = 2 * m + r
            v_heads[m, e, r] = v_rows[pl.ds(h, length, stride=value_heads), :].astype(BF16)
        gates[m, e] = jnp.concatenate([g[2 * m:2 * m + 2], b[2 * m:2 * m + 2], spare], axis=0)


def prepare_group(group, chunk, ids, q_heads, k_heads, gates, t_ref, m_ref, aux_ref, a_rows):
    length = q_heads.shape[2]
    value_heads = 2 * len(ids)
    row = lax.broadcasted_iota(jnp.int32, (length, length), 0)
    col = lax.broadcasted_iota(jnp.int32, (length, length), 1)
    inclusive = row >= col
    strict = row > col
    diagonal = row == col
    ones_low = inclusive.astype(F32).astype(BF16)
    ones_up = (row <= col).astype(F32).astype(BF16)
    eye = diagonal.astype(F32).astype(BF16)
    picked = [gates[chunk, e] for e in ids]
    g_narrow = jnp.concatenate([gate[0:2] for gate in picked], axis=0).astype(BF16)
    b_narrow = jnp.concatenate([gate[2:4] for gate in picked], axis=0).astype(BF16)
    g_col = dot_nt(ones_low, g_narrow)
    g_row = dot(g_narrow, ones_up)
    b = dot_nt(eye, b_narrow)
    lane = lax.broadcasted_iota(jnp.int32, (BASE, length), 1)
    sub = lax.broadcasted_iota(jnp.int32, (BASE, length), 0)
    parts = length // BASE
    unit_cols = []
    compact = []
    for m, e in enumerate(ids):
        q = q_heads[chunk, e]
        k = k_heads[chunk, e]
        both = dot_nt(jnp.concatenate([k, q], axis=0), k)
        kk = both[:length]
        qk = both[length:]
        squares = jnp.where(diagonal, kk, 0.0)
        n_row = lax.rsqrt(jnp.sum(squares, axis=0, keepdims=True) + norm_epsilon)
        n_col = lax.rsqrt(jnp.sum(squares, axis=1, keepdims=True) + norm_epsilon)
        unit_cols += [n_col, n_col]
        kk = kk * n_row * n_col
        qk = qk * n_row
        for r in range(2):
            h = 2 * m + r
            decay = jnp.exp(jnp.where(inclusive, g_col[:, h:h + 1] - g_row[h:h + 1, :], 0.0))
            m_ref[group, h] = jnp.where(inclusive, qk * decay, 0.0)
            a = jnp.where(strict, kk * decay * b[:, h:h + 1], 0.0)
            a_rows[h] = a
            piece = jnp.zeros((BASE, length), F32)
            for p in range(parts):
                piece = jnp.where(lane // BASE == p, a[p * BASE:(p + 1) * BASE], piece)
            compact.append(piece)
    inverses = [(lane % BASE == sub).astype(F32) for _ in range(value_heads)]
    for j in range(BASE - 1):
        index = (lane // BASE) * BASE + j
        for h in range(value_heads):
            factor = jnp.take_along_axis(compact[h], index, axis=1)
            inverses[h] = inverses[h] - factor * inverses[h][j:j + 1, :]
    block_masks = [lane // BASE == p for p in range(parts)]
    levels = []
    size = BASE
    while size < length:
        levels.append((size, range(size, length, 2 * size)))
        size *= 2
    heads = range(value_heads)
    for h in heads:
        blocks = [jnp.where(block_masks[p], inverses[h], 0.0) for p in range(parts)]
        t_ref[group, h] = jnp.concatenate(blocks, axis=0)
    for size, starts in levels:
        columns = lax.broadcasted_iota(jnp.int32, (size, length), 1) // size
        empty = jnp.zeros((size, length), F32)
        steps = []
        for h in heads:
            lower = [
                jnp.where(columns == start // size - 1, a_rows[h, start:start + size, :], 0.0)
                for start in starts
            ]
            steps.append(dot3(jnp.concatenate(lower, axis=0), t_ref[group, h]))
        for h in heads:
            spread = []
            for n in range(len(starts)):
                spread += [empty, steps[h][n * size:(n + 1) * size]]
            odd = jnp.concatenate(
                [t_ref[group, h, start:start + size, :] for start in starts], axis=0
            )
            odd = odd - dot3(odd, jnp.concatenate(spread, axis=0))
            for n, start in enumerate(starts):
                t_ref[group, h, start:start + size, :] = odd[n * size:(n + 1) * size]
    units = jnp.concatenate(unit_cols, axis=1)
    growth = jnp.exp(g_col)
    rest = jnp.exp(g_col[length - 1:length, :] - g_col) * units
    aux_ref[group] = jnp.concatenate([growth, b, b * growth * units, rest], axis=1)


def advance_group(group, chunk, ids, lives, owners, slots, q_heads, k_heads, v_heads, t_ref, m_ref,
                  aux_ref, gain, states, stage, o_rows):
    length, key_dim = q_heads.shape[2:]
    width = v_heads.shape[-1]
    value_heads = 2 * len(ids)
    all_heads = 2 * q_heads.shape[0]
    aux = aux_ref[group]
    columns = lambda n, h: aux[:, n * value_heads + h:n * value_heads + h + 1]
    half = lambda pair, r: pair[:, r * width:(r + 1) * width]
    token = lax.broadcasted_iota(jnp.int32, (length, width), 0)
    keys, applied = [], []
    for m, e in enumerate(ids):
        q = q_heads[chunk, e]
        k = k_heads[chunk, e]
        s_high, s_low = split(states[owners[m], slots[m]])
        kq = jnp.concatenate([k, q], axis=0)
        keys.append(k)
        applied.append(
            dot(jnp.concatenate([kq, kq], axis=1), jnp.concatenate([s_high, s_low], axis=0))
        )
    fixed = []
    for h in range(value_heads):
        v = v_heads[chunk, ids[h // 2], h % 2].astype(F32)
        right = columns(1, h) * v - columns(2, h) * half(applied[h // 2][:length], h % 2)
        fixed.append(dot3(t_ref[group, h], right))
    powers = []
    for m, e in enumerate(ids):
        k = keys[m]
        update = jnp.concatenate(
            [columns(3, 2 * m + r) * fixed[2 * m + r] for r in range(2)], axis=1
        )
        u_high, u_low = split(update)
        added = dot_tn(jnp.concatenate([k, k], axis=0), jnp.concatenate([u_high, u_low], axis=0))
        state = states[owners[m], slots[m]]
        later = []
        for r in range(2):
            last = aux[length - 1:length, 2 * m + r:2 * m + r + 1]
            later.append(last * half(state, r) + half(added, r))
        word, pair_powers = code_pair(later)
        stage[chunk, group, m * key_dim:(m + 1) * key_dim, :] = word
        powers += pair_powers
    stage[chunk, group, len(ids) * key_dim:, :] = stack_powers(powers)
    for h in range(value_heads):
        out = columns(0, h) * half(applied[h // 2][length:], h % 2)
        out = out + dot3(m_ref[group, h], fixed[h])
        mean_square = jnp.mean(out * out, axis=1, keepdims=True)
        normed = out * lax.rsqrt(mean_square + norm_epsilon) * gain
        rows = pl.ds(2 * chunk + h % 2, length, stride=all_heads)
        o_rows[group * len(ids) + h // 2, rows, :] = jnp.where(token < lives[h // 2], normed, 0.0)


def exchange_kernel(order_ref, owner_ref, slot_ref, count_ref, gain_ref, g_ref, b_ref, q_any, k_any,
                    v_any, parents_any, mixed, codes, parents, q_raw, k_raw, v_raw, q_rows,
                    k_rows, v_rows, q_heads, k_heads, v_heads, gates, t_ref, m_ref, aux_ref, a_rows,
                    blocks, scales, states, stage, o_rows, parent_sem, raw_sem, line_send,
                    line_recv, final_send, final_recv):
    ring = lax.axis_size("seq")
    me = lax.axis_index("seq")
    chunks, expansions = q_heads.shape[:2]
    groups = ring
    per_peer = expansions // ring

    def parent_copy(c):
        return pltpu.make_async_copy(
            parents_any.at[:, 2 * c:2 * c + 2], parents.at[c], parent_sem.at[c]
        )

    def raw_copies(e):
        pairs = ((q_any, q_raw), (k_any, k_raw), (v_any, v_raw))
        return [
            pltpu.make_async_copy(a.at[e], b.at[e], raw_sem.at[e, n])
            for n, (a, b) in enumerate(pairs)
        ]

    def line_copies(c, way, hop, source, peer):
        return [
            pltpu.make_async_remote_copy(
                src_ref=held.at[c, source],
                dst_ref=held.at[c, source],
                send_sem=line_send.at[c, way, hop, n],
                recv_sem=line_recv.at[c, way, hop, n],
                device_id={"seq": peer},
                device_id_type=MESH,
            )
            for n, held in enumerate((scales, blocks))
        ]

    def line_start(c):
        @pl.when(me < ring - 1)
        def _():
            for copy in line_copies(c, 0, 0, me, me + 1):
                copy.start()

        @pl.when(me > 0)
        def _():
            for copy in line_copies(c, 1, 0, me, me - 1):
                copy.start()

    def line_hop(c, hop):
        for way, step in ((0, 1), (1, -1)):
            source = me - step * hop
            inside = (source >= 0) & (source <= ring - 1)
            onward = inside & (me + step >= 0) & (me + step <= ring - 1)

            @pl.when(inside)
            def _():
                for copy in line_copies(c, way, hop - 1, source, me - step):
                    copy.wait_recv()

            @pl.when(onward)
            def _():
                for copy in line_copies(c, way, hop, source, me + step):
                    copy.start()

    def line_drain(c, hop):
        for way, step in ((0, 1), (1, -1)):
            source = me - step * hop
            inside = (source >= 0) & (source <= ring - 1)
            onward = inside & (me + step >= 0) & (me + step <= ring - 1)

            @pl.when(onward)
            def _():
                for copy in line_copies(c, way, hop, source, me + step):
                    copy.wait_send()

    def final_copy(c, i, source, peer):
        return pltpu.make_async_remote_copy(
            src_ref=stage.at[c, i],
            dst_ref=codes.at[c, source],
            send_sem=final_send.at[c, i],
            recv_sem=final_recv.at[c, i],
            device_id={"seq": peer},
            device_id_type=MESH,
        )

    def own_copy(c):
        return pltpu.make_async_copy(
            stage.at[c, groups - 1], codes.at[c, me], final_send.at[c, groups - 1]
        )

    def members(i):
        first = lax.rem(me + turn(ring, i), ring) * expansions + me * per_peer
        return [order_ref[first + a] for a in range(per_peer)]

    for c in range(chunks):
        parent_copy(c).start()
    barrier = pltpu.get_barrier_semaphore()
    for i in range(1, ring):
        pl.semaphore_signal(
            barrier, inc=1, device_id={"seq": lax.rem(me + i, ring)}, device_id_type=MESH
        )
    parent_copy(0).wait()
    encode_chunk(parents, blocks, scales, 0, me)
    pl.semaphore_wait(barrier, ring - 1)
    line_start(0)

    @pl.loop(0, expansions)
    def _(e):
        for copy in raw_copies(e):
            copy.start()

    for c in range(1, chunks):
        parent_copy(c).wait()
        encode_chunk(parents, blocks, scales, c, me)
        if c == 1:
            line_start(1)

    @pl.loop(0, expansions)
    def _(e):
        for copy in raw_copies(e):
            copy.wait()
        unpack_expansion(e, count_ref[me * expansions + e], q_raw, k_raw, v_raw, g_ref, b_ref,
                         q_rows, k_rows, v_rows, q_heads, k_heads, v_heads, gates)

    line_hop(0, 1)
    gain = gain_ref[...].astype(F32)

    @pl.loop(0, chunks)
    def _(c):
        def tick(t):
            @pl.when(c + 1 < chunks)
            def _():
                @pl.when((t == 2) & (c + 2 < chunks))
                def _():
                    line_start(c + 2)

                @pl.when((t > 1) & (t % 2 == 1) & (t // 2 < ring - 1))
                def _():
                    line_hop(c + 1, t // 2)

        @pl.loop(0, groups)
        def _(i):
            tick(i)

            @pl.when((c == 0) & (i > 1) & (i < ring - 1))
            def _():
                line_hop(0, i)

            ids = [jnp.maximum(number - me * expansions, 0) for number in members(i)]
            prepare_group(i, c, ids, q_heads, k_heads, gates, t_ref, m_ref, aux_ref, a_rows)

        line_hop(c, ring - 1)

        @pl.loop(0, ring)
        def _(source):
            decode_chunk(c, source, blocks, scales, states)

        @pl.loop(0, groups)
        def _(i):
            tick(groups + i)
            numbers = members(i)
            ids = [jnp.maximum(number - me * expansions, 0) for number in numbers]
            lives = [count_ref[number] for number in numbers]
            owners = [owner_ref[number] for number in numbers]
            slots = [slot_ref[number] for number in numbers]
            advance_group(i, c, ids, lives, owners, slots, q_heads, k_heads, v_heads, t_ref, m_ref,
                          aux_ref, gain, states, stage, o_rows)

            @pl.when(i < groups - 1)
            def _():
                final_copy(c, i, me, lax.rem(me + turn(ring, i), ring)).start()

            @pl.when(i == groups - 1)
            def _():
                own_copy(c).start()

            @pl.when(c == chunks - 1)
            def _():
                for a in range(per_peer):
                    j = i * per_peer + a
                    mixed[j] = o_rows[j].astype(BF16)

    @pl.loop(0, chunks)
    def _(c):
        own_copy(c).wait()

        @pl.loop(0, ring - 1)
        def _(hop):
            line_drain(c, hop)

        @pl.loop(0, groups - 1)
        def _(i):
            source = lax.rem(me + ring - turn(ring, i), ring)
            copy = final_copy(c, i, source, lax.rem(me + turn(ring, i), ring))
            copy.wait_send()
            copy.wait_recv()


def exchange(order, owner, slot, count, gain, decay, rate, queries, keys, values, parents, ring):
    expansions, rows, key_dim = queries.shape
    cached, value_heads, _, width = parents.shape
    chunks = value_heads // 2
    length = rows // chunks
    per_peer = expansions // ring
    heads = 2 * per_peer
    final_rows = per_peer * key_dim + padded_rows(2 * per_peer)
    anywhere = pl.BlockSpec(memory_space=pl.ANY)
    whole = pl.BlockSpec(memory_space=pltpu.VMEM)
    scalars = pl.BlockSpec(memory_space=pltpu.SMEM)
    work = expansions * value_heads
    return pl.pallas_call(
        exchange_kernel,
        out_shape=(
            pltpu.VMEM(values.shape, BF16),
            pltpu.VMEM((chunks, ring, final_rows, width), jnp.int32),
        ),
        in_specs=[scalars] * 4 + [whole] * 3 + [anywhere] * 4,
        out_specs=(whole, whole),
        scratch_shapes=[
            pltpu.VMEM((chunks, cached, 2, key_dim, width), F32),
            pltpu.VMEM(queries.shape, BF16),
            pltpu.VMEM(keys.shape, BF16),
            pltpu.VMEM(values.shape, BF16),
            pltpu.VMEM((rows, key_dim), F32),
            pltpu.VMEM((rows, key_dim), F32),
            pltpu.VMEM((length * value_heads, width), F32),
            pltpu.VMEM((chunks, expansions, length, key_dim), BF16),
            pltpu.VMEM((chunks, expansions, length, key_dim), BF16),
            pltpu.VMEM((chunks, expansions, 2, length, width), BF16),
            pltpu.VMEM((chunks, expansions, 8, length), F32),
            pltpu.VMEM((ring, heads, length, length), F32),
            pltpu.VMEM((ring, heads, length, length), F32),
            pltpu.VMEM((ring, length, 4 * heads), F32),
            pltpu.VMEM((heads, length, length), F32),
            pltpu.VMEM((chunks, ring, cached, key_dim, width), jnp.int32),
            pltpu.VMEM((chunks, ring, padded_rows(2 * cached), width), jnp.int32),
            pltpu.VMEM((ring, cached, key_dim, 2 * width), F32),
            pltpu.VMEM((chunks, ring, final_rows, width), jnp.int32),
            pltpu.VMEM(values.shape, F32),
            pltpu.SemaphoreType.DMA((chunks,)),
            pltpu.SemaphoreType.DMA((expansions, 3)),
            pltpu.SemaphoreType.DMA((chunks, 2, ring - 1, 2)),
            pltpu.SemaphoreType.DMA((chunks, 2, ring - 1, 2)),
            pltpu.SemaphoreType.DMA((chunks, ring)),
            pltpu.SemaphoreType.DMA((chunks, ring)),
        ],
        compiler_params=pltpu.CompilerParams(
            vmem_limit_bytes=EXCHANGE_BYTES, collective_id=0, has_side_effects=True
        ),
        cost_estimate=pl.CostEstimate(
            flops=work * 40 * length**3,
            bytes_accessed=work * length**2 * 16,
            transcendentals=work * length**2,
        ),
        name="exchange",
    )(order, owner, slot, count, gain, decay, rate, queries, keys, values, parents)


def finish_kernel(ring, order_ref, codes_ref, slots_ref, state_ref, mixed_any, sems):
    step = pl.program_id(0)
    me = lax.axis_index("seq")
    per_peer, value_heads, key_dim, _ = state_ref.shape
    expansions = ring * per_peer

    def leave(i, a):
        j = i * per_peer + a
        first = lax.rem(me + turn(ring, i), ring) * expansions + me * per_peer
        number = order_ref[first + a] - me * expansions
        return pltpu.make_async_copy(slots_ref.at[j], mixed_any.at[number], sems.at[j])

    for a in range(per_peer):
        leave(step, a).start()

    for c in range(value_heads // 2):
        scales = jnp.exp2(codes_ref[c, step, per_peer * key_dim:, :].astype(F32))
        for a in range(per_peer):
            word = codes_ref[c, step, a * key_dim:(a + 1) * key_dim, :]
            pair = [scales[2 * a + r:2 * a + r + 1, :] for r in range(2)]
            state_ref[a, 2 * c], state_ref[a, 2 * c + 1] = decode_pair(word, pair)

    @pl.when(step == ring - 1)
    def _():
        for i in range(ring):
            for a in range(per_peer):
                leave(i, a).wait()


def finish(order, codes, slots, state_shape, ring):
    expansions, value_heads, key_dim, width = state_shape
    per_peer = expansions // ring
    return pl.pallas_call(
        functools.partial(finish_kernel, ring),
        out_shape=(
            jax.ShapeDtypeStruct(state_shape, F32),
            jax.ShapeDtypeStruct(slots.shape, BF16),
        ),
        grid_spec=pltpu.PrefetchScalarGridSpec(
            num_scalar_prefetch=1,
            grid=(ring,),
            in_specs=[pl.BlockSpec(memory_space=pltpu.VMEM), pl.BlockSpec(memory_space=pltpu.VMEM)],
            out_specs=(
                pl.BlockSpec((per_peer, value_heads, key_dim, width), lambda i, order: (i, 0, 0, 0)),
                pl.BlockSpec(memory_space=pl.ANY),
            ),
            scratch_shapes=[pltpu.SemaphoreType.DMA((expansions,))],
        ),
        compiler_params=pltpu.CompilerParams(vmem_limit_bytes=VMEM_BYTES),
        name="finish",
    )(
        order,
        pltpu.with_memory_space_constraint(codes, pltpu.VMEM),
        pltpu.with_memory_space_constraint(slots, pltpu.VMEM),
    )


def shards(queries, keys, values, log_decay, write_rate, norm_gain, parent_cache, order,
           parent_owner, parent_slot, token_count):
    ring = lax.axis_size("seq")
    expansions, length, key_heads, key_dim = queries.shape
    value_heads = 2 * key_heads
    width = values.shape[-1]
    cached = parent_cache.shape[0]
    turned = lambda x: x.transpose(0, 2, 3, 1).reshape(expansions, value_heads, length)
    slots, codes = exchange(
        order,
        parent_owner,
        parent_slot,
        token_count,
        norm_gain.reshape(1, width),
        turned(log_decay),
        turned(write_rate),
        queries.reshape(expansions, length * key_heads, key_dim),
        keys.reshape(expansions, length * key_heads, key_dim),
        values.reshape(expansions, length * value_heads, width),
        parent_cache.reshape(cached, value_heads, key_dim, width),
        ring,
    )
    final, mixed = finish(order, codes, slots, (expansions, value_heads, key_dim, width), ring)
    return (
        mixed.reshape(values.shape),
        final.reshape((expansions,) + parent_cache.shape[1:]),
    )


def solution(mesh):
    heads = ("head", "sub")
    rows = ("groups", "seq")
    placed = (
        P(rows, None, heads, None),
        P(rows, None, heads, None),
        P(rows, None, heads, None, None),
        P(rows, None, heads, None),
        P(rows, None, heads, None),
        P(),
        P(rows, heads, None, None, None),
        P("groups"),
        P("groups"),
        P("groups"),
        P("groups"),
    )
    return jax.shard_map(
        shards,
        mesh=mesh,
        in_specs=placed,
        out_specs=(P(rows, None, heads, None, None), P(rows, heads, None, None, None)),
        check_vma=False,
    )
```

```python
import functools

import jax
import jax.numpy as jnp
from jax import lax
from jax.experimental import pallas as pl
from jax.experimental.pallas import tpu as pltpu
from jax.sharding import PartitionSpec as P

norm_epsilon = 1e-06
BASE = 16
F32 = jnp.float32
BF16 = jnp.bfloat16
EXCHANGE_BYTES = 42 * 1024 * 1024
FINISH_BYTES = 8 * 1024 * 1024


def split(x):
    high = x.astype(BF16)
    low = (x - high.astype(F32)).astype(BF16)
    return high, low


def dot(a, b):
    return jnp.dot(a, b, preferred_element_type=F32)


def dot_nt(a, b):
    return lax.dot_general(a, b, (((1,), (1,)), ((), ())), preferred_element_type=F32)


def dot_tn(a, b):
    return lax.dot_general(a, b, (((0,), (0,)), ((), ())), preferred_element_type=F32)


def dot3(a, b):
    a_high, a_low = split(a)
    b_high, b_low = split(b)
    right = jnp.concatenate([b_high, b_low], axis=1)
    both = dot(jnp.concatenate([a_high, a_low], axis=1), jnp.concatenate([right, right], axis=0))
    width = b.shape[1]
    return both[:, :width] + both[:, width:]


CODE_BITS = 15
RAW_SLOTS = 4
MESH = pl.DeviceIdType.MESH


def turn(ring, i):
    far = lax.div(i + 1, 2)
    return ring // 2 + jnp.where(lax.rem(i, 2) == 1, -far, far)


def code_state(state):
    largest = jnp.maximum(jnp.max(jnp.abs(state), axis=0, keepdims=True), 1e-30)
    power = jnp.ceil(jnp.log2(largest)) - CODE_BITS
    limit = float(2**CODE_BITS - 1)
    code = jnp.clip(jnp.round(state * jnp.exp2(-power)), -limit, limit)
    return code.astype(jnp.int32), power.astype(jnp.int32)


def pack_pair(low, high):
    return (high << 16) | (low & 0xFFFF)


def unpack_pair(word):
    return [(word << 16) >> 16, word >> 16]


def code_pair(states):
    (low, low_power), (high, high_power) = [code_state(state) for state in states]
    return pack_pair(low, high), pack_pair(low_power, high_power)


def decode_pair(word, powers):
    scales = [jnp.exp2(power.astype(F32)) for power in unpack_pair(powers)]
    return [code.astype(F32) * scale for code, scale in zip(unpack_pair(word), scales)]


def encode_chunk(parents, blocks, scales, chunk, me):
    count = parents.shape[1]
    powers = []
    for i in range(count):
        word, pair_powers = code_pair([parents[chunk, i, 0], parents[chunk, i, 1]])
        blocks[chunk, me, i] = word
        powers.append(pair_powers)
    scales[chunk, me] = jnp.concatenate(powers, axis=0)


def decode_chunk(chunk, source, blocks, scales, states):
    count, _, width = blocks.shape[2:]
    powers = scales[chunk, source]
    for i in range(count):
        pair = decode_pair(blocks[chunk, source, i], powers[i:i + 1, :])
        for r in range(2):
            states[source, i, :, r * width:(r + 1) * width] = pair[r]


def decode_finals(codes, finals, first, head):
    rows = finals.shape[-2]
    count = codes.shape[0] // (rows + 1)
    powers = codes[count * rows:, :]
    for a in range(count):
        pair = decode_pair(codes[a * rows:(a + 1) * rows, :], powers[a:a + 1, :])
        for r in range(2):
            finals[first + a, head + r] = pair[r]


def unpack_expansion(e, slot, live, q_raw, k_raw, v_raw, g_ref, b_ref, q_rows, k_rows, v_rows, q_heads,
                     k_heads, v_heads, gates):
    key_heads, _, length, _ = q_heads.shape
    value_heads = 2 * key_heads
    q_rows[...] = q_raw[slot].astype(F32)
    k_rows[...] = k_raw[slot].astype(F32)
    v_rows[...] = v_raw[slot].astype(F32)
    alive = lax.broadcasted_iota(jnp.int32, (value_heads, length), 1) < live
    g = jnp.where(alive, g_ref[e].astype(F32), 0.0)
    b = jnp.where(alive, b_ref[e].astype(F32), 0.0)
    spare = jnp.zeros((4, length), F32)
    for m in range(key_heads):
        q_heads[m, e] = q_rows[pl.ds(m, length, stride=key_heads), :].astype(BF16)
        k_heads[m, e] = k_rows[pl.ds(m, length, stride=key_heads), :].astype(BF16)
        for r in range(2):
            h = 2 * m + r
            v_heads[m, e, r] = v_rows[pl.ds(h, length, stride=value_heads), :].astype(BF16)
        gates[m, e] = jnp.concatenate([g[2 * m:2 * m + 2], b[2 * m:2 * m + 2], spare], axis=0)


def prepare_group(group, chunk, ids, q_heads, k_heads, gates, t_ref, m_ref, aux_ref, a_rows):
    length = q_heads.shape[2]
    value_heads = 2 * len(ids)
    row = lax.broadcasted_iota(jnp.int32, (length, length), 0)
    col = lax.broadcasted_iota(jnp.int32, (length, length), 1)
    inclusive = row >= col
    strict = row > col
    diagonal = row == col
    ones_low = inclusive.astype(F32).astype(BF16)
    ones_up = (row <= col).astype(F32).astype(BF16)
    eye = diagonal.astype(F32).astype(BF16)
    picked = [gates[chunk, e] for e in ids]
    g_narrow = jnp.concatenate([gate[0:2] for gate in picked], axis=0).astype(BF16)
    b_narrow = jnp.concatenate([gate[2:4] for gate in picked], axis=0).astype(BF16)
    g_col = dot_nt(ones_low, g_narrow)
    g_row = dot(g_narrow, ones_up)
    b = dot_nt(eye, b_narrow)
    lane = lax.broadcasted_iota(jnp.int32, (BASE, length), 1)
    sub = lax.broadcasted_iota(jnp.int32, (BASE, length), 0)
    parts = length // BASE
    unit_cols = []
    compact = []
    for m, e in enumerate(ids):
        q = q_heads[chunk, e]
        k = k_heads[chunk, e]
        both = dot_nt(jnp.concatenate([k, q], axis=0), k)
        kk = both[:length]
        qk = both[length:]
        squares = jnp.where(diagonal, kk, 0.0)
        n_row = lax.rsqrt(jnp.sum(squares, axis=0, keepdims=True) + norm_epsilon)
        n_col = lax.rsqrt(jnp.sum(squares, axis=1, keepdims=True) + norm_epsilon)
        unit_cols += [n_col, n_col]
        kk = kk * n_row * n_col
        qk = qk * n_row
        for r in range(2):
            h = 2 * m + r
            decay = jnp.exp(jnp.where(inclusive, g_col[:, h:h + 1] - g_row[h:h + 1, :], 0.0))
            m_ref[group, h] = jnp.where(inclusive, qk * decay, 0.0)
            a = jnp.where(strict, kk * decay * b[:, h:h + 1], 0.0)
            a_rows[h] = a
            piece = jnp.zeros((BASE, length), F32)
            for p in range(parts):
                piece = jnp.where(lane // BASE == p, a[p * BASE:(p + 1) * BASE], piece)
            compact.append(piece)
    inverses = [(lane % BASE == sub).astype(F32) for _ in range(value_heads)]
    for j in range(BASE - 1):
        index = (lane // BASE) * BASE + j
        for h in range(value_heads):
            factor = jnp.take_along_axis(compact[h], index, axis=1)
            inverses[h] = inverses[h] - factor * inverses[h][j:j + 1, :]
    block_masks = [lane // BASE == p for p in range(parts)]
    levels = []
    size = BASE
    while size < length:
        levels.append((size, range(size, length, 2 * size)))
        size *= 2
    heads = range(value_heads)
    for h in heads:
        blocks = [jnp.where(block_masks[p], inverses[h], 0.0) for p in range(parts)]
        t_ref[group, h] = jnp.concatenate(blocks, axis=0)
    for size, starts in levels:
        columns = lax.broadcasted_iota(jnp.int32, (size, length), 1) // size
        empty = jnp.zeros((size, length), F32)
        steps = []
        for h in heads:
            lower = [
                jnp.where(columns == start // size - 1, a_rows[h, start:start + size, :], 0.0)
                for start in starts
            ]
            steps.append(dot3(jnp.concatenate(lower, axis=0), t_ref[group, h]))
        for h in heads:
            spread = []
            for n in range(len(starts)):
                spread += [empty, steps[h][n * size:(n + 1) * size]]
            odd = jnp.concatenate(
                [t_ref[group, h, start:start + size, :] for start in starts], axis=0
            )
            odd = odd - dot3(odd, jnp.concatenate(spread, axis=0))
            for n, start in enumerate(starts):
                t_ref[group, h, start:start + size, :] = odd[n * size:(n + 1) * size]
    units = jnp.concatenate(unit_cols, axis=1)
    growth = jnp.exp(g_col)
    rest = jnp.exp(g_col[length - 1:length, :] - g_col) * units
    aux_ref[group] = jnp.concatenate([growth, b, b * growth * units, rest], axis=1)


def advance_group(group, chunk, ids, lives, owners, slots, q_heads, k_heads, v_heads, t_ref, m_ref,
                  aux_ref, gain, states, stage, o_rows):
    length, key_dim = q_heads.shape[2:]
    width = v_heads.shape[-1]
    value_heads = 2 * len(ids)
    all_heads = 2 * q_heads.shape[0]
    aux = aux_ref[group]
    columns = lambda n, h: aux[:, n * value_heads + h:n * value_heads + h + 1]
    half = lambda pair, r: pair[:, r * width:(r + 1) * width]
    token = lax.broadcasted_iota(jnp.int32, (length, width), 0)
    keys, applied = [], []
    for m, e in enumerate(ids):
        q = q_heads[chunk, e]
        k = k_heads[chunk, e]
        s_high, s_low = split(states[owners[m], slots[m]])
        kq = jnp.concatenate([k, q], axis=0)
        keys.append(k)
        applied.append(
            dot(jnp.concatenate([kq, kq], axis=1), jnp.concatenate([s_high, s_low], axis=0))
        )
    fixed = []
    for h in range(value_heads):
        v = v_heads[chunk, ids[h // 2], h % 2].astype(F32)
        right = columns(1, h) * v - columns(2, h) * half(applied[h // 2][:length], h % 2)
        fixed.append(dot3(t_ref[group, h], right))
    powers = []
    for m, e in enumerate(ids):
        k = keys[m]
        update = jnp.concatenate(
            [columns(3, 2 * m + r) * fixed[2 * m + r] for r in range(2)], axis=1
        )
        u_high, u_low = split(update)
        added = dot_tn(jnp.concatenate([k, k], axis=0), jnp.concatenate([u_high, u_low], axis=0))
        state = states[owners[m], slots[m]]
        later = []
        for r in range(2):
            last = aux[length - 1:length, 2 * m + r:2 * m + r + 1]
            later.append(last * half(state, r) + half(added, r))
        word, pair_powers = code_pair(later)
        stage[chunk, group, m * key_dim:(m + 1) * key_dim, :] = word
        powers.append(pair_powers)
    stage[chunk, group, len(ids) * key_dim:, :] = jnp.concatenate(powers, axis=0)
    for h in range(value_heads):
        out = columns(0, h) * half(applied[h // 2][length:], h % 2)
        out = out + dot3(m_ref[group, h], fixed[h])
        mean_square = jnp.mean(out * out, axis=1, keepdims=True)
        normed = out * lax.rsqrt(mean_square + norm_epsilon) * gain
        rows = pl.ds(2 * chunk + h % 2, length, stride=all_heads)
        o_rows[group * len(ids) + h // 2, rows, :] = jnp.where(token < lives[h // 2], normed, 0.0)


def exchange_kernel(order_ref, owner_ref, slot_ref, count_ref, gain_ref, g_ref, b_ref, q_any, k_any,
                    v_any, parents_any, mixed, codes, early, parents, q_raw, k_raw, v_raw, q_rows,
                    k_rows, v_rows, q_heads, k_heads, v_heads, gates, t_ref, m_ref, aux_ref, a_rows,
                    blocks, scales, states, stage, o_rows, parent_sem, raw_sem, line_send,
                    line_recv, final_send, final_recv):
    ring = lax.axis_size("seq")
    me = lax.axis_index("seq")
    chunks, expansions = q_heads.shape[:2]
    groups = ring
    depth = q_raw.shape[0]
    per_peer = expansions // ring

    def parent_copy(c):
        return pltpu.make_async_copy(
            parents_any.at[:, 2 * c:2 * c + 2], parents.at[c], parent_sem.at[c]
        )

    def raw_copies(e):
        pairs = ((q_any, q_raw), (k_any, k_raw), (v_any, v_raw))
        slot = lax.rem(e, depth)
        return [
            pltpu.make_async_copy(a.at[e], b.at[slot], raw_sem.at[slot, n])
            for n, (a, b) in enumerate(pairs)
        ]

    def line_copies(c, way, hop, source, peer):
        return [
            pltpu.make_async_remote_copy(
                src_ref=held.at[c, source],
                dst_ref=held.at[c, source],
                send_sem=line_send.at[c, way, hop, n],
                recv_sem=line_recv.at[c, way, hop, n],
                device_id={"seq": peer},
                device_id_type=MESH,
            )
            for n, held in enumerate((scales, blocks))
        ]

    def line_start(c):
        @pl.when(me < ring - 1)
        def _():
            for copy in line_copies(c, 0, 0, me, me + 1):
                copy.start()

        @pl.when(me > 0)
        def _():
            for copy in line_copies(c, 1, 0, me, me - 1):
                copy.start()

    def line_hop(c, hop):
        for way, step in ((0, 1), (1, -1)):
            source = me - step * hop
            inside = (source >= 0) & (source <= ring - 1)
            onward = inside & (me + step >= 0) & (me + step <= ring - 1)

            @pl.when(inside)
            def _():
                for copy in line_copies(c, way, hop - 1, source, me - step):
                    copy.wait_recv()

            @pl.when(onward)
            def _():
                for copy in line_copies(c, way, hop, source, me + step):
                    copy.start()

    def line_drain(c, hop):
        for way, step in ((0, 1), (1, -1)):
            source = me - step * hop
            inside = (source >= 0) & (source <= ring - 1)
            onward = inside & (me + step >= 0) & (me + step <= ring - 1)

            @pl.when(onward)
            def _():
                for copy in line_copies(c, way, hop, source, me + step):
                    copy.wait_send()

    def final_copy(c, i, source, peer):
        return pltpu.make_async_remote_copy(
            src_ref=stage.at[c, i],
            dst_ref=codes.at[c, source],
            send_sem=final_send.at[c, i],
            recv_sem=final_recv.at[c, i],
            device_id={"seq": peer},
            device_id_type=MESH,
        )

    def own_copy(c):
        return pltpu.make_async_copy(
            stage.at[c, groups - 1], codes.at[c, me], final_send.at[c, groups - 1]
        )

    def members(i):
        first = lax.rem(me + turn(ring, i), ring) * expansions + me * per_peer
        return [order_ref[first + a] for a in range(per_peer)]

    for c in range(chunks):
        parent_copy(c).start()
    barrier = pltpu.get_barrier_semaphore()
    for i in range(1, ring):
        pl.semaphore_signal(
            barrier, inc=1, device_id={"seq": lax.rem(me + i, ring)}, device_id_type=MESH
        )
    parent_copy(0).wait()
    encode_chunk(parents, blocks, scales, 0, me)
    pl.semaphore_wait(barrier, ring - 1)
    line_start(0)

    @pl.loop(0, depth)
    def _(e):
        for copy in raw_copies(e):
            copy.start()

    for c in range(1, chunks):
        parent_copy(c).wait()
        encode_chunk(parents, blocks, scales, c, me)
        if c == 1:
            line_start(1)

    @pl.loop(0, expansions)
    def _(e):
        for copy in raw_copies(e):
            copy.wait()
        unpack_expansion(e, lax.rem(e, depth), count_ref[me * expansions + e], q_raw, k_raw, v_raw, g_ref, b_ref,
                         q_rows, k_rows, v_rows, q_heads, k_heads, v_heads, gates)

        @pl.when(e + depth < expansions)
        def _():
            for copy in raw_copies(e + depth):
                copy.start()

    line_hop(0, 1)
    gain = gain_ref[...].astype(F32)

    @pl.loop(0, chunks)
    def _(c):
        def tick(t):
            @pl.when(c + 1 < chunks)
            def _():
                @pl.when((t == 2) & (c + 2 < chunks))
                def _():
                    line_start(c + 2)

                @pl.when((t > 1) & (t % 2 == 1) & (t // 2 < ring - 1))
                def _():
                    line_hop(c + 1, t // 2)

        @pl.loop(0, groups)
        def _(i):
            tick(i)

            @pl.when((c == 0) & (i > 1) & (i < ring - 1))
            def _():
                line_hop(0, i)

            ids = [jnp.maximum(number - me * expansions, 0) for number in members(i)]
            prepare_group(i, c, ids, q_heads, k_heads, gates, t_ref, m_ref, aux_ref, a_rows)

        line_hop(c, ring - 1)

        @pl.loop(0, ring)
        def _(source):
            decode_chunk(c, source, blocks, scales, states)

        @pl.loop(0, groups)
        def _(i):
            tick(groups + i)
            numbers = members(i)
            ids = [jnp.maximum(number - me * expansions, 0) for number in numbers]
            lives = [count_ref[number] for number in numbers]
            owners = [owner_ref[number] for number in numbers]
            slots = [slot_ref[number] for number in numbers]
            advance_group(i, c, ids, lives, owners, slots, q_heads, k_heads, v_heads, t_ref, m_ref,
                          aux_ref, gain, states, stage, o_rows)

            @pl.when(i < groups - 1)
            def _():
                final_copy(c, i, me, lax.rem(me + turn(ring, i), ring)).start()

            @pl.when(i == groups - 1)
            def _():
                own_copy(c).start()

            @pl.when(c == chunks - 1)
            def _():
                for a in range(per_peer):
                    j = i * per_peer + a
                    mixed[j] = o_rows[j].astype(BF16)

    @pl.loop(0, chunks)
    def _(c):
        own_copy(c).wait()

        @pl.loop(0, ring - 1)
        def _(hop):
            line_drain(c, hop)

        @pl.loop(0, groups - 1)
        def _(i):
            source = lax.rem(me + ring - turn(ring, i), ring)
            copy = final_copy(c, i, source, lax.rem(me + turn(ring, i), ring))
            copy.wait_send()
            copy.wait_recv()

            @pl.when(c < chunks - 1)
            def _():
                decode_finals(codes.at[c, source], early, source * per_peer, 2 * c)

        @pl.when(c < chunks - 1)
        def _():
            decode_finals(codes.at[c, me], early, me * per_peer, 2 * c)


def exchange(order, owner, slot, count, gain, decay, rate, queries, keys, values, parents, ring):
    expansions, rows, key_dim = queries.shape
    cached, value_heads, _, width = parents.shape
    chunks = value_heads // 2
    length = rows // chunks
    per_peer = expansions // ring
    heads = 2 * per_peer
    depth = min(RAW_SLOTS, expansions)
    final_rows = per_peer * (key_dim + 1)
    anywhere = pl.BlockSpec(memory_space=pl.ANY)
    whole = pl.BlockSpec(memory_space=pltpu.VMEM)
    scalars = pl.BlockSpec(memory_space=pltpu.SMEM)
    work = expansions * value_heads
    return pl.pallas_call(
        exchange_kernel,
        out_shape=(
            pltpu.VMEM(values.shape, BF16),
            pltpu.VMEM((chunks, ring, final_rows, width), jnp.int32),
            pltpu.VMEM((expansions, value_heads - 2, key_dim, width), F32),
        ),
        in_specs=[scalars] * 4 + [whole] * 3 + [anywhere] * 4,
        out_specs=(whole, whole, whole),
        scratch_shapes=[
            pltpu.VMEM((chunks, cached, 2, key_dim, width), F32),
            pltpu.VMEM((depth,) + queries.shape[1:], BF16),
            pltpu.VMEM((depth,) + keys.shape[1:], BF16),
            pltpu.VMEM((depth,) + values.shape[1:], BF16),
            pltpu.VMEM((rows, key_dim), F32),
            pltpu.VMEM((rows, key_dim), F32),
            pltpu.VMEM((length * value_heads, width), F32),
            pltpu.VMEM((chunks, expansions, length, key_dim), BF16),
            pltpu.VMEM((chunks, expansions, length, key_dim), BF16),
            pltpu.VMEM((chunks, expansions, 2, length, width), BF16),
            pltpu.VMEM((chunks, expansions, 8, length), F32),
            pltpu.VMEM((ring, heads, length, length), F32),
            pltpu.VMEM((ring, heads, length, length), F32),
            pltpu.VMEM((ring, length, 4 * heads), F32),
            pltpu.VMEM((heads, length, length), F32),
            pltpu.VMEM((chunks, ring, cached, key_dim, width), jnp.int32),
            pltpu.VMEM((chunks, ring, cached, width), jnp.int32),
            pltpu.VMEM((ring, cached, key_dim, 2 * width), F32),
            pltpu.VMEM((chunks, ring, final_rows, width), jnp.int32),
            pltpu.VMEM(values.shape, F32),
            pltpu.SemaphoreType.DMA((chunks,)),
            pltpu.SemaphoreType.DMA((depth, 3)),
            pltpu.SemaphoreType.DMA((chunks, 2, ring - 1, 2)),
            pltpu.SemaphoreType.DMA((chunks, 2, ring - 1, 2)),
            pltpu.SemaphoreType.DMA((chunks, ring)),
            pltpu.SemaphoreType.DMA((chunks, ring)),
        ],
        compiler_params=pltpu.CompilerParams(
            vmem_limit_bytes=EXCHANGE_BYTES, collective_id=0, has_side_effects=True
        ),
        cost_estimate=pl.CostEstimate(
            flops=work * 40 * length**3,
            bytes_accessed=work * length**2 * 16,
            transcendentals=work * length**2,
        ),
        name="exchange",
    )(order, owner, slot, count, gain, decay, rate, queries, keys, values, parents)


def finish_kernel(ring, order_ref, slots_ref, codes_ref, early_ref, final_any, mixed_any, late,
                  slot_sem, early_sem, late_sem):
    me = lax.axis_index("seq")
    expansions = late.shape[0]
    head = early_ref.shape[1]
    per_peer = expansions // ring
    copies = []
    for j in range(expansions):
        copies.append(
            pltpu.make_async_copy(early_ref.at[j], final_any.at[j, 0:head], early_sem.at[j])
        )
    for i in range(ring):
        first = lax.rem(me + turn(ring, i), ring) * expansions + me * per_peer
        for a in range(per_peer):
            j = i * per_peer + a
            number = order_ref[first + a] - me * expansions
            copies.append(
                pltpu.make_async_copy(slots_ref.at[j], mixed_any.at[number], slot_sem.at[j])
            )
    for copy in copies:
        copy.start()
    for source in range(ring):
        decode_finals(codes_ref.at[codes_ref.shape[0] - 1, source], late, source * per_peer, 0)
        for j in range(source * per_peer, (source + 1) * per_peer):
            copy = pltpu.make_async_copy(
                late.at[j], final_any.at[j, head:head + 2], late_sem.at[j]
            )
            copy.start()
            copies.append(copy)
    for copy in copies:
        copy.wait()


def finish(order, slots, codes, early, ring):
    expansions, early_heads, key_dim, width = early.shape
    whole = pl.BlockSpec(memory_space=pltpu.VMEM)
    anywhere = pl.BlockSpec(memory_space=pl.ANY)
    return pl.pallas_call(
        functools.partial(finish_kernel, ring),
        out_shape=(
            jax.ShapeDtypeStruct((expansions, early_heads + 2, key_dim, width), F32),
            jax.ShapeDtypeStruct(slots.shape, BF16),
        ),
        in_specs=[pl.BlockSpec(memory_space=pltpu.SMEM), whole, whole, whole],
        out_specs=(anywhere, anywhere),
        scratch_shapes=[
            pltpu.VMEM((expansions, 2, key_dim, width), F32),
            pltpu.SemaphoreType.DMA((expansions,)),
            pltpu.SemaphoreType.DMA((expansions,)),
            pltpu.SemaphoreType.DMA((expansions,)),
        ],
        compiler_params=pltpu.CompilerParams(vmem_limit_bytes=FINISH_BYTES),
        name="finish",
    )(order, *[pltpu.with_memory_space_constraint(x, pltpu.VMEM) for x in (slots, codes, early)])


def shards(queries, keys, values, log_decay, write_rate, norm_gain, parent_cache, order,
           parent_owner, parent_slot, token_count):
    ring = lax.axis_size("seq")
    expansions, length, key_heads, key_dim = queries.shape
    value_heads = 2 * key_heads
    width = values.shape[-1]
    cached = parent_cache.shape[0]
    turned = lambda x: x.transpose(0, 2, 3, 1).reshape(expansions, value_heads, length)
    slots, codes, early = exchange(
        order,
        parent_owner,
        parent_slot,
        token_count,
        norm_gain.reshape(1, width),
        turned(log_decay),
        turned(write_rate),
        queries.reshape(expansions, length * key_heads, key_dim),
        keys.reshape(expansions, length * key_heads, key_dim),
        values.reshape(expansions, length * value_heads, width),
        parent_cache.reshape(cached, value_heads, key_dim, width),
        ring,
    )
    final, mixed = finish(order, slots, codes, early, ring)
    return (
        mixed.reshape(values.shape),
        final.reshape((expansions,) + parent_cache.shape[1:]),
    )


def solution(mesh):
    heads = ("head", "sub")
    rows = ("groups", "seq")
    placed = (
        P(rows, None, heads, None),
        P(rows, None, heads, None),
        P(rows, None, heads, None, None),
        P(rows, None, heads, None),
        P(rows, None, heads, None),
        P(),
        P(rows, heads, None, None, None),
        P("groups"),
        P("groups"),
        P("groups"),
        P("groups"),
    )
    return jax.shard_map(
        shards,
        mesh=mesh,
        in_specs=placed,
        out_specs=(P(rows, None, heads, None, None), P(rows, heads, None, None, None)),
        check_vma=False,
    )
```

```python
import functools

import jax
import jax.numpy as jnp
from jax import lax
from jax.experimental import pallas as pl
from jax.experimental.pallas import tpu as pltpu
from jax.sharding import PartitionSpec as P

norm_epsilon = 1e-06
BASE = 16
F32 = jnp.float32
BF16 = jnp.bfloat16
EXCHANGE_BYTES = 42 * 1024 * 1024
FINISH_BYTES = 8 * 1024 * 1024


def split(x):
    high = x.astype(BF16)
    low = (x - high.astype(F32)).astype(BF16)
    return high, low


def dot(a, b):
    return jnp.dot(a, b, preferred_element_type=F32)


def dot_nt(a, b):
    return lax.dot_general(a, b, (((1,), (1,)), ((), ())), preferred_element_type=F32)


def dot_tn(a, b):
    return lax.dot_general(a, b, (((0,), (0,)), ((), ())), preferred_element_type=F32)


def dot3(a, b):
    a_high, a_low = split(a)
    b_high, b_low = split(b)
    right = jnp.concatenate([b_high, b_low], axis=1)
    both = dot(jnp.concatenate([a_high, a_low], axis=1), jnp.concatenate([right, right], axis=0))
    width = b.shape[1]
    return both[:, :width] + both[:, width:]


CODE_BITS = 15
RAW_SLOTS = 4
MESH = pl.DeviceIdType.MESH


def turn(ring, i):
    far = lax.div(i + 1, 2)
    return ring // 2 + jnp.where(lax.rem(i, 2) == 1, -far, far)


def code_state(state):
    largest = jnp.maximum(jnp.max(jnp.abs(state), axis=0, keepdims=True), 1e-30)
    power = jnp.ceil(jnp.log2(largest)) - CODE_BITS
    limit = float(2**CODE_BITS - 1)
    code = jnp.clip(jnp.round(state * jnp.exp2(-power)), -limit, limit)
    return code.astype(jnp.int32), power.astype(jnp.int32)


def pack_pair(low, high):
    return (high << 16) | (low & 0xFFFF)


def unpack_pair(word):
    return [(word << 16) >> 16, word >> 16]


def code_pair(states):
    (low, low_power), (high, high_power) = [code_state(state) for state in states]
    return pack_pair(low, high), pack_pair(low_power, high_power)


def decode_pair(word, powers):
    scales = [jnp.exp2(power.astype(F32)) for power in unpack_pair(powers)]
    return [code.astype(F32) * scale for code, scale in zip(unpack_pair(word), scales)]


def encode_chunk(parents, blocks, scales, chunk, me, before=None, after=None):
    count = parents.shape[1]
    powers = []
    for i in range(count):
        if before:
            before(i)
        word, pair_powers = code_pair([parents[chunk, i, 0], parents[chunk, i, 1]])
        blocks[chunk, me, i] = word
        powers.append(pair_powers)
        if after:
            after(i)
    scales[chunk, me] = jnp.concatenate(powers, axis=0)


def decode_chunk(chunk, source, blocks, scales, states):
    count, _, width = blocks.shape[2:]
    powers = scales[chunk, source]
    for i in range(count):
        pair = decode_pair(blocks[chunk, source, i], powers[i:i + 1, :])
        for r in range(2):
            states[source, i, :, r * width:(r + 1) * width] = pair[r]


def decode_finals(codes, finals, first, head):
    rows = finals.shape[-2]
    count = codes.shape[0] // (rows + 1)
    powers = codes[count * rows:, :]
    for a in range(count):
        pair = decode_pair(codes[a * rows:(a + 1) * rows, :], powers[a:a + 1, :])
        for r in range(2):
            finals[first + a, head + r] = pair[r]


def unpack_expansion(e, slot, live, q_raw, k_raw, v_raw, g_ref, b_ref, q_rows, k_rows, v_rows, q_heads,
                     k_heads, v_heads, gates):
    key_heads, _, length, _ = q_heads.shape
    value_heads = 2 * key_heads
    q_rows[...] = q_raw[slot].astype(F32)
    k_rows[...] = k_raw[slot].astype(F32)
    v_rows[...] = v_raw[slot].astype(F32)
    alive = lax.broadcasted_iota(jnp.int32, (value_heads, length), 1) < live
    g = jnp.where(alive, g_ref[e].astype(F32), 0.0)
    b = jnp.where(alive, b_ref[e].astype(F32), 0.0)
    spare = jnp.zeros((4, length), F32)
    for m in range(key_heads):
        q_heads[m, e] = q_rows[pl.ds(m, length, stride=key_heads), :].astype(BF16)
        k_heads[m, e] = k_rows[pl.ds(m, length, stride=key_heads), :].astype(BF16)
        for r in range(2):
            h = 2 * m + r
            v_heads[m, e, r] = v_rows[pl.ds(h, length, stride=value_heads), :].astype(BF16)
        gates[m, e] = jnp.concatenate([g[2 * m:2 * m + 2], b[2 * m:2 * m + 2], spare], axis=0)


def prepare_group(group, chunk, ids, q_heads, k_heads, gates, t_ref, m_ref, aux_ref, a_rows):
    length = q_heads.shape[2]
    value_heads = 2 * len(ids)
    row = lax.broadcasted_iota(jnp.int32, (length, length), 0)
    col = lax.broadcasted_iota(jnp.int32, (length, length), 1)
    inclusive = row >= col
    strict = row > col
    diagonal = row == col
    ones_low = inclusive.astype(F32).astype(BF16)
    ones_up = (row <= col).astype(F32).astype(BF16)
    eye = diagonal.astype(F32).astype(BF16)
    picked = [gates[chunk, e] for e in ids]
    g_narrow = jnp.concatenate([gate[0:2] for gate in picked], axis=0).astype(BF16)
    b_narrow = jnp.concatenate([gate[2:4] for gate in picked], axis=0).astype(BF16)
    g_col = dot_nt(ones_low, g_narrow)
    g_row = dot(g_narrow, ones_up)
    b = dot_nt(eye, b_narrow)
    lane = lax.broadcasted_iota(jnp.int32, (BASE, length), 1)
    sub = lax.broadcasted_iota(jnp.int32, (BASE, length), 0)
    parts = length // BASE
    unit_cols = []
    compact = []
    for m, e in enumerate(ids):
        q = q_heads[chunk, e]
        k = k_heads[chunk, e]
        both = dot_nt(jnp.concatenate([k, q], axis=0), k)
        kk = both[:length]
        qk = both[length:]
        squares = jnp.where(diagonal, kk, 0.0)
        n_row = lax.rsqrt(jnp.sum(squares, axis=0, keepdims=True) + norm_epsilon)
        n_col = lax.rsqrt(jnp.sum(squares, axis=1, keepdims=True) + norm_epsilon)
        unit_cols += [n_col, n_col]
        kk = kk * n_row * n_col
        qk = qk * n_row
        for r in range(2):
            h = 2 * m + r
            decay = jnp.exp(jnp.where(inclusive, g_col[:, h:h + 1] - g_row[h:h + 1, :], 0.0))
            m_ref[group, h] = jnp.where(inclusive, qk * decay, 0.0)
            a = jnp.where(strict, kk * decay * b[:, h:h + 1], 0.0)
            a_rows[h] = a
            piece = jnp.zeros((BASE, length), F32)
            for p in range(parts):
                piece = jnp.where(lane // BASE == p, a[p * BASE:(p + 1) * BASE], piece)
            compact.append(piece)
    inverses = [(lane % BASE == sub).astype(F32) for _ in range(value_heads)]
    for j in range(BASE - 1):
        index = (lane // BASE) * BASE + j
        for h in range(value_heads):
            factor = jnp.take_along_axis(compact[h], index, axis=1)
            inverses[h] = inverses[h] - factor * inverses[h][j:j + 1, :]
    block_masks = [lane // BASE == p for p in range(parts)]
    levels = []
    size = BASE
    while size < length:
        levels.append((size, range(size, length, 2 * size)))
        size *= 2
    heads = range(value_heads)
    for h in heads:
        blocks = [jnp.where(block_masks[p], inverses[h], 0.0) for p in range(parts)]
        t_ref[group, h] = jnp.concatenate(blocks, axis=0)
    for size, starts in levels:
        columns = lax.broadcasted_iota(jnp.int32, (size, length), 1) // size
        empty = jnp.zeros((size, length), F32)
        steps = []
        for h in heads:
            lower = [
                jnp.where(columns == start // size - 1, a_rows[h, start:start + size, :], 0.0)
                for start in starts
            ]
            steps.append(dot3(jnp.concatenate(lower, axis=0), t_ref[group, h]))
        for h in heads:
            spread = []
            for n in range(len(starts)):
                spread += [empty, steps[h][n * size:(n + 1) * size]]
            odd = jnp.concatenate(
                [t_ref[group, h, start:start + size, :] for start in starts], axis=0
            )
            odd = odd - dot3(odd, jnp.concatenate(spread, axis=0))
            for n, start in enumerate(starts):
                t_ref[group, h, start:start + size, :] = odd[n * size:(n + 1) * size]
    units = jnp.concatenate(unit_cols, axis=1)
    growth = jnp.exp(g_col)
    rest = jnp.exp(g_col[length - 1:length, :] - g_col) * units
    aux_ref[group] = jnp.concatenate([growth, b, b * growth * units, rest], axis=1)


def advance_group(group, chunk, ids, lives, owners, slots, q_heads, k_heads, v_heads, t_ref, m_ref,
                  aux_ref, gain, states, stage, o_rows):
    length, key_dim = q_heads.shape[2:]
    width = v_heads.shape[-1]
    value_heads = 2 * len(ids)
    all_heads = 2 * q_heads.shape[0]
    aux = aux_ref[group]
    columns = lambda n, h: aux[:, n * value_heads + h:n * value_heads + h + 1]
    half = lambda pair, r: pair[:, r * width:(r + 1) * width]
    token = lax.broadcasted_iota(jnp.int32, (length, width), 0)
    keys, applied = [], []
    for m, e in enumerate(ids):
        q = q_heads[chunk, e]
        k = k_heads[chunk, e]
        s_high, s_low = split(states[owners[m], slots[m]])
        kq = jnp.concatenate([k, q], axis=0)
        keys.append(k)
        applied.append(
            dot(jnp.concatenate([kq, kq], axis=1), jnp.concatenate([s_high, s_low], axis=0))
        )
    fixed = []
    for h in range(value_heads):
        v = v_heads[chunk, ids[h // 2], h % 2].astype(F32)
        right = columns(1, h) * v - columns(2, h) * half(applied[h // 2][:length], h % 2)
        fixed.append(dot3(t_ref[group, h], right))
    powers = []
    for m, e in enumerate(ids):
        k = keys[m]
        update = jnp.concatenate(
            [columns(3, 2 * m + r) * fixed[2 * m + r] for r in range(2)], axis=1
        )
        u_high, u_low = split(update)
        added = dot_tn(jnp.concatenate([k, k], axis=0), jnp.concatenate([u_high, u_low], axis=0))
        state = states[owners[m], slots[m]]
        later = []
        for r in range(2):
            last = aux[length - 1:length, 2 * m + r:2 * m + r + 1]
            later.append(last * half(state, r) + half(added, r))
        word, pair_powers = code_pair(later)
        stage[chunk, group, m * key_dim:(m + 1) * key_dim, :] = word
        powers.append(pair_powers)
    stage[chunk, group, len(ids) * key_dim:, :] = jnp.concatenate(powers, axis=0)
    for h in range(value_heads):
        out = columns(0, h) * half(applied[h // 2][length:], h % 2)
        out = out + dot3(m_ref[group, h], fixed[h])
        mean_square = jnp.mean(out * out, axis=1, keepdims=True)
        normed = out * lax.rsqrt(mean_square + norm_epsilon) * gain
        rows = pl.ds(2 * chunk + h % 2, length, stride=all_heads)
        o_rows[group * len(ids) + h // 2, rows, :] = jnp.where(token < lives[h // 2], normed, 0.0)


def exchange_kernel(order_ref, owner_ref, slot_ref, count_ref, gain_ref, g_ref, b_ref, q_any, k_any,
                    v_any, parents_any, mixed, codes, early, parents, q_raw, k_raw, v_raw, q_rows,
                    k_rows, v_rows, q_heads, k_heads, v_heads, gates, t_ref, m_ref, aux_ref, a_rows,
                    blocks, scales, states, stage, o_rows, first_sem, parent_sem, raw_sem, line_send,
                    line_recv, final_send, final_recv):
    ring = lax.axis_size("seq")
    me = lax.axis_index("seq")
    chunks, expansions = q_heads.shape[:2]
    groups = ring
    depth = q_raw.shape[0]
    per_peer = expansions // ring

    def parent_copy(c):
        return pltpu.make_async_copy(
            parents_any.at[:, 2 * c:2 * c + 2], parents.at[c], parent_sem.at[c]
        )

    def raw_copies(e):
        pairs = ((q_any, q_raw), (k_any, k_raw), (v_any, v_raw))
        slot = lax.rem(e, depth)
        return [
            pltpu.make_async_copy(a.at[e], b.at[slot], raw_sem.at[slot, n])
            for n, (a, b) in enumerate(pairs)
        ]

    def line_copies(c, way, hop, source, peer):
        return [
            pltpu.make_async_remote_copy(
                src_ref=held.at[c, source],
                dst_ref=held.at[c, source],
                send_sem=line_send.at[c, way, hop, n],
                recv_sem=line_recv.at[c, way, hop, n],
                device_id={"seq": peer},
                device_id_type=MESH,
            )
            for n, held in enumerate((scales, blocks))
        ]

    def first_copy(i):
        return pltpu.make_async_copy(
            parents_any.at[i, 0:2], parents.at[0, i], first_sem.at[i]
        )

    def first_send(i):
        if i == 0:
            pl.semaphore_wait(barrier, ring - 1)
        held = blocks.at[0, me, i] if i < blocks.shape[2] else scales.at[0, me]
        kind = 1 if i < blocks.shape[2] else 0
        for way, step in ((0, 1), (1, -1)):
            @pl.when((me + step >= 0) & (me + step <= ring - 1))
            def _():
                pltpu.make_async_remote_copy(
                    src_ref=held,
                    dst_ref=held,
                    send_sem=line_send.at[0, way, 0, kind],
                    recv_sem=line_recv.at[0, way, 0, kind],
                    device_id={"seq": me + step},
                    device_id_type=MESH,
                ).start()

    def line_start(c):
        @pl.when(me < ring - 1)
        def _():
            for copy in line_copies(c, 0, 0, me, me + 1):
                copy.start()

        @pl.when(me > 0)
        def _():
            for copy in line_copies(c, 1, 0, me, me - 1):
                copy.start()

    def line_hop(c, hop):
        for way, step in ((0, 1), (1, -1)):
            source = me - step * hop
            inside = (source >= 0) & (source <= ring - 1)
            onward = inside & (me + step >= 0) & (me + step <= ring - 1)

            @pl.when(inside)
            def _():
                for copy in line_copies(c, way, hop - 1, source, me - step):
                    copy.wait_recv()

            @pl.when(onward)
            def _():
                for copy in line_copies(c, way, hop, source, me + step):
                    copy.start()

    def line_drain(c, hop):
        for way, step in ((0, 1), (1, -1)):
            source = me - step * hop
            inside = (source >= 0) & (source <= ring - 1)
            onward = inside & (me + step >= 0) & (me + step <= ring - 1)

            @pl.when(onward)
            def _():
                for copy in line_copies(c, way, hop, source, me + step):
                    copy.wait_send()

    def final_copy(c, i, source, peer):
        return pltpu.make_async_remote_copy(
            src_ref=stage.at[c, i],
            dst_ref=codes.at[c, source],
            send_sem=final_send.at[c, i],
            recv_sem=final_recv.at[c, i],
            device_id={"seq": peer},
            device_id_type=MESH,
        )

    def own_copy(c):
        return pltpu.make_async_copy(
            stage.at[c, groups - 1], codes.at[c, me], final_send.at[c, groups - 1]
        )

    def members(i):
        first = lax.rem(me + turn(ring, i), ring) * expansions + me * per_peer
        return [order_ref[first + a] for a in range(per_peer)]

    for i in range(blocks.shape[2]):
        first_copy(i).start()
    barrier = pltpu.get_barrier_semaphore()
    for i in range(1, ring):
        pl.semaphore_signal(
            barrier, inc=1, device_id={"seq": lax.rem(me + i, ring)}, device_id_type=MESH
        )
    encode_chunk(parents, blocks, scales, 0, me, lambda i: first_copy(i).wait(), first_send)
    first_send(blocks.shape[2])
    for c in range(1, chunks):
        parent_copy(c).start()

    @pl.loop(0, depth)
    def _(e):
        for copy in raw_copies(e):
            copy.start()

    for c in range(1, chunks):
        parent_copy(c).wait()
        encode_chunk(parents, blocks, scales, c, me)
        if c == 1:
            line_start(1)

    @pl.loop(0, expansions)
    def _(e):
        for copy in raw_copies(e):
            copy.wait()
        unpack_expansion(e, lax.rem(e, depth), count_ref[me * expansions + e], q_raw, k_raw, v_raw, g_ref, b_ref,
                         q_rows, k_rows, v_rows, q_heads, k_heads, v_heads, gates)

        @pl.when(e + depth < expansions)
        def _():
            for copy in raw_copies(e + depth):
                copy.start()

    line_hop(0, 1)
    gain = gain_ref[...].astype(F32)

    @pl.loop(0, chunks)
    def _(c):
        def tick(t):
            @pl.when(c + 1 < chunks)
            def _():
                @pl.when((t == 2) & (c + 2 < chunks))
                def _():
                    line_start(c + 2)

                @pl.when((t > 1) & (t % 2 == 1) & (t // 2 < ring - 1))
                def _():
                    line_hop(c + 1, t // 2)

        @pl.loop(0, groups)
        def _(i):
            tick(i)

            @pl.when((c == 0) & (i > 1) & (i < ring - 1))
            def _():
                line_hop(0, i)

            ids = [jnp.maximum(number - me * expansions, 0) for number in members(i)]
            prepare_group(i, c, ids, q_heads, k_heads, gates, t_ref, m_ref, aux_ref, a_rows)

        line_hop(c, ring - 1)

        @pl.loop(0, ring)
        def _(source):
            decode_chunk(c, source, blocks, scales, states)

        @pl.loop(0, groups)
        def _(i):
            tick(groups + i)
            numbers = members(i)
            ids = [jnp.maximum(number - me * expansions, 0) for number in numbers]
            lives = [count_ref[number] for number in numbers]
            owners = [owner_ref[number] for number in numbers]
            slots = [slot_ref[number] for number in numbers]
            advance_group(i, c, ids, lives, owners, slots, q_heads, k_heads, v_heads, t_ref, m_ref,
                          aux_ref, gain, states, stage, o_rows)

            @pl.when(i < groups - 1)
            def _():
                final_copy(c, i, me, lax.rem(me + turn(ring, i), ring)).start()

            @pl.when(i == groups - 1)
            def _():
                own_copy(c).start()

    @pl.loop(0, expansions)
    def _(e):
        row = 0
        for i in range(groups):
            for a, number in enumerate(members(i)):
                here = number == me * expansions + e
                row = jnp.maximum(row, jnp.where(here, i * per_peer + a, 0))
        mixed[e] = o_rows[row].astype(BF16)

    @pl.loop(0, chunks)
    def _(c):
        own_copy(c).wait()

        @pl.loop(0, ring - 1)
        def _(hop):
            line_drain(c, hop)

        @pl.loop(0, groups - 1)
        def _(i):
            source = lax.rem(me + ring - turn(ring, i), ring)
            copy = final_copy(c, i, source, lax.rem(me + turn(ring, i), ring))
            copy.wait_send()
            copy.wait_recv()

            @pl.when(c < chunks - 1)
            def _():
                decode_finals(codes.at[c, source], early, source * per_peer, 2 * c)

        @pl.when(c < chunks - 1)
        def _():
            decode_finals(codes.at[c, me], early, me * per_peer, 2 * c)


def exchange(order, owner, slot, count, gain, decay, rate, queries, keys, values, parents, ring):
    expansions, rows, key_dim = queries.shape
    cached, value_heads, _, width = parents.shape
    chunks = value_heads // 2
    length = rows // chunks
    per_peer = expansions // ring
    heads = 2 * per_peer
    depth = min(RAW_SLOTS, expansions)
    final_rows = per_peer * (key_dim + 1)
    anywhere = pl.BlockSpec(memory_space=pl.ANY)
    whole = pl.BlockSpec(memory_space=pltpu.VMEM)
    scalars = pl.BlockSpec(memory_space=pltpu.SMEM)
    work = expansions * value_heads
    return pl.pallas_call(
        exchange_kernel,
        out_shape=(
            pltpu.VMEM(values.shape, BF16),
            pltpu.VMEM((chunks, ring, final_rows, width), jnp.int32),
            pltpu.VMEM((expansions, value_heads - 2, key_dim, width), F32),
        ),
        in_specs=[scalars] * 4 + [whole] * 3 + [anywhere] * 4,
        out_specs=(whole, whole, whole),
        scratch_shapes=[
            pltpu.VMEM((chunks, cached, 2, key_dim, width), F32),
            pltpu.VMEM((depth,) + queries.shape[1:], BF16),
            pltpu.VMEM((depth,) + keys.shape[1:], BF16),
            pltpu.VMEM((depth,) + values.shape[1:], BF16),
            pltpu.VMEM((rows, key_dim), F32),
            pltpu.VMEM((rows, key_dim), F32),
            pltpu.VMEM((length * value_heads, width), F32),
            pltpu.VMEM((chunks, expansions, length, key_dim), BF16),
            pltpu.VMEM((chunks, expansions, length, key_dim), BF16),
            pltpu.VMEM((chunks, expansions, 2, length, width), BF16),
            pltpu.VMEM((chunks, expansions, 8, length), F32),
            pltpu.VMEM((ring, heads, length, length), F32),
            pltpu.VMEM((ring, heads, length, length), F32),
            pltpu.VMEM((ring, length, 4 * heads), F32),
            pltpu.VMEM((heads, length, length), F32),
            pltpu.VMEM((chunks, ring, cached, key_dim, width), jnp.int32),
            pltpu.VMEM((chunks, ring, cached, width), jnp.int32),
            pltpu.VMEM((ring, cached, key_dim, 2 * width), F32),
            pltpu.VMEM((chunks, ring, final_rows, width), jnp.int32),
            pltpu.VMEM(values.shape, F32),
            pltpu.SemaphoreType.DMA((cached,)),
            pltpu.SemaphoreType.DMA((chunks,)),
            pltpu.SemaphoreType.DMA((depth, 3)),
            pltpu.SemaphoreType.DMA((chunks, 2, ring - 1, 2)),
            pltpu.SemaphoreType.DMA((chunks, 2, ring - 1, 2)),
            pltpu.SemaphoreType.DMA((chunks, ring)),
            pltpu.SemaphoreType.DMA((chunks, ring)),
        ],
        compiler_params=pltpu.CompilerParams(
            vmem_limit_bytes=EXCHANGE_BYTES, collective_id=0, has_side_effects=True
        ),
        cost_estimate=pl.CostEstimate(
            flops=work * 40 * length**3,
            bytes_accessed=work * length**2 * 16,
            transcendentals=work * length**2,
        ),
        name="exchange",
    )(order, owner, slot, count, gain, decay, rate, queries, keys, values, parents)


def finish_kernel(mixed_ref, codes_ref, early_ref, final_any, mixed_any, late, mixed_sem, early_sem,
                  late_sem):
    chunks, ring = codes_ref.shape[:2]
    per_peer = late.shape[0] // ring
    head = early_ref.shape[1]
    group = lambda source: pl.ds(source * per_peer, per_peer)
    copies = [pltpu.make_async_copy(mixed_ref, mixed_any, mixed_sem)]
    for source in range(ring):
        copies.append(
            pltpu.make_async_copy(
                early_ref.at[group(source)],
                final_any.at[group(source), 0:head],
                early_sem.at[source],
            )
        )
    for copy in copies:
        copy.start()
    for source in range(ring):
        decode_finals(codes_ref.at[chunks - 1, source], late, source * per_peer, 0)
        copy = pltpu.make_async_copy(
            late.at[group(source)], final_any.at[group(source), head:head + 2], late_sem.at[source]
        )
        copy.start()
        copies.append(copy)
    for copy in copies:
        copy.wait()


def finish(mixed, codes, early, ring):
    expansions, early_heads, key_dim, width = early.shape
    whole = pl.BlockSpec(memory_space=pltpu.VMEM)
    anywhere = pl.BlockSpec(memory_space=pl.ANY)
    return pl.pallas_call(
        finish_kernel,
        out_shape=(
            jax.ShapeDtypeStruct((expansions, early_heads + 2, key_dim, width), F32),
            jax.ShapeDtypeStruct(mixed.shape, BF16),
        ),
        in_specs=[whole, whole, whole],
        out_specs=(anywhere, anywhere),
        scratch_shapes=[
            pltpu.VMEM((expansions, 2, key_dim, width), F32),
            pltpu.SemaphoreType.DMA,
            pltpu.SemaphoreType.DMA((ring,)),
            pltpu.SemaphoreType.DMA((ring,)),
        ],
        compiler_params=pltpu.CompilerParams(vmem_limit_bytes=FINISH_BYTES),
        name="finish",
    )(*[pltpu.with_memory_space_constraint(x, pltpu.VMEM) for x in (mixed, codes, early)])


def shards(queries, keys, values, log_decay, write_rate, norm_gain, parent_cache, order,
           parent_owner, parent_slot, token_count):
    ring = lax.axis_size("seq")
    expansions, length, key_heads, key_dim = queries.shape
    value_heads = 2 * key_heads
    width = values.shape[-1]
    cached = parent_cache.shape[0]
    turned = lambda x: x.transpose(0, 2, 3, 1).reshape(expansions, value_heads, length)
    mixed, codes, early = exchange(
        order,
        parent_owner,
        parent_slot,
        token_count,
        norm_gain.reshape(1, width),
        turned(log_decay),
        turned(write_rate),
        queries.reshape(expansions, length * key_heads, key_dim),
        keys.reshape(expansions, length * key_heads, key_dim),
        values.reshape(expansions, length * value_heads, width),
        parent_cache.reshape(cached, value_heads, key_dim, width),
        ring,
    )
    final, mixed = finish(mixed, codes, early, ring)
    return (
        mixed.reshape(values.shape),
        final.reshape((expansions,) + parent_cache.shape[1:]),
    )


def solution(mesh):
    heads = ("head", "sub")
    rows = ("groups", "seq")
    placed = (
        P(rows, None, heads, None),
        P(rows, None, heads, None),
        P(rows, None, heads, None, None),
        P(rows, None, heads, None),
        P(rows, None, heads, None),
        P(),
        P(rows, heads, None, None, None),
        P("groups"),
        P("groups"),
        P("groups"),
        P("groups"),
    )
    return jax.shard_map(
        shards,
        mesh=mesh,
        in_specs=placed,
        out_specs=(P(rows, None, heads, None, None), P(rows, heads, None, None, None)),
        check_vma=False,
    )
```

```python
import functools

import jax
import jax.numpy as jnp
from jax import lax
from jax.experimental import pallas as pl
from jax.experimental.pallas import tpu as pltpu
from jax.sharding import PartitionSpec as P

norm_epsilon = 1e-06
BASE = 16
F32 = jnp.float32
BF16 = jnp.bfloat16
EXCHANGE_BYTES = 42 * 1024 * 1024
FINISH_BYTES = 8 * 1024 * 1024


def split(x):
    high = x.astype(BF16)
    low = (x - high.astype(F32)).astype(BF16)
    return high, low


def dot(a, b):
    return jnp.dot(a, b, preferred_element_type=F32)


def dot_nt(a, b):
    return lax.dot_general(a, b, (((1,), (1,)), ((), ())), preferred_element_type=F32)


def dot_tn(a, b):
    return lax.dot_general(a, b, (((0,), (0,)), ((), ())), preferred_element_type=F32)


def dot3(a, b):
    a_high, a_low = split(a)
    b_high, b_low = split(b)
    right = jnp.concatenate([b_high, b_low], axis=1)
    both = dot(jnp.concatenate([a_high, a_low], axis=1), jnp.concatenate([right, right], axis=0))
    width = b.shape[1]
    return both[:, :width] + both[:, width:]


CODE_BITS = 15
RAW_SLOTS = 4
MESH = pl.DeviceIdType.MESH


def turn(ring, i):
    far = lax.div(i + 1, 2)
    return ring // 2 + jnp.where(lax.rem(i, 2) == 1, -far, far)


def code_state(state):
    largest = jnp.maximum(jnp.max(jnp.abs(state), axis=0, keepdims=True), 1e-30)
    power = jnp.ceil(jnp.log2(largest)) - CODE_BITS
    limit = float(2**CODE_BITS - 1)
    code = jnp.clip(jnp.round(state * jnp.exp2(-power)), -limit, limit)
    return code.astype(jnp.int32), power.astype(jnp.int32)


def pack_pair(low, high):
    return (high << 16) | (low & 0xFFFF)


def unpack_pair(word):
    return [(word << 16) >> 16, word >> 16]


def code_pair(states):
    (low, low_power), (high, high_power) = [code_state(state) for state in states]
    return pack_pair(low, high), pack_pair(low_power, high_power)


def decode_pair(word, powers):
    scales = [jnp.exp2(power.astype(F32)) for power in unpack_pair(powers)]
    return [code.astype(F32) * scale for code, scale in zip(unpack_pair(word), scales)]


def encode_chunk(parents, blocks, scales, chunk, me, before=None, after=None):
    count = parents.shape[1]
    powers = []
    for i in range(count):
        if before:
            before(i)
        word, pair_powers = code_pair([parents[chunk, i, 0], parents[chunk, i, 1]])
        blocks[chunk, me, i] = word
        powers.append(pair_powers)
        if after:
            after(i)
    scales[chunk, me] = jnp.concatenate(powers, axis=0)


def decode_chunk(chunk, source, blocks, scales, states):
    count, _, width = blocks.shape[2:]
    powers = scales[chunk, source]
    for i in range(count):
        pair = decode_pair(blocks[chunk, source, i], powers[i:i + 1, :])
        for r in range(2):
            states[source, i, :, r * width:(r + 1) * width] = pair[r]


def decode_finals(codes, finals, first, head):
    rows = finals.shape[-2]
    count = codes.shape[0] // (rows + 1)
    powers = codes[count * rows:, :]
    for a in range(count):
        pair = decode_pair(codes[a * rows:(a + 1) * rows, :], powers[a:a + 1, :])
        for r in range(2):
            finals[first + a, head + r] = pair[r]


def unpack_expansion(e, slot, live, q_raw, k_raw, v_raw, g_ref, b_ref, q_rows, k_rows, v_rows, q_heads,
                     k_heads, v_heads, gates):
    key_heads, _, length, _ = q_heads.shape
    value_heads = 2 * key_heads
    q_rows[...] = q_raw[slot].astype(F32)
    k_rows[...] = k_raw[slot].astype(F32)
    v_rows[...] = v_raw[slot].astype(F32)
    alive = lax.broadcasted_iota(jnp.int32, (value_heads, length), 1) < live
    g = jnp.where(alive, g_ref[e].astype(F32), 0.0)
    b = jnp.where(alive, b_ref[e].astype(F32), 0.0)
    spare = jnp.zeros((4, length), F32)
    for m in range(key_heads):
        q_heads[m, e] = q_rows[pl.ds(m, length, stride=key_heads), :].astype(BF16)
        k_heads[m, e] = k_rows[pl.ds(m, length, stride=key_heads), :].astype(BF16)
        for r in range(2):
            h = 2 * m + r
            v_heads[m, e, r] = v_rows[pl.ds(h, length, stride=value_heads), :].astype(BF16)
        gates[m, e] = jnp.concatenate([g[2 * m:2 * m + 2], b[2 * m:2 * m + 2], spare], axis=0)


def prepare_group(group, chunk, ids, q_heads, k_heads, gates, t_ref, m_ref, aux_ref, a_rows):
    length = q_heads.shape[2]
    value_heads = 2 * len(ids)
    row = lax.broadcasted_iota(jnp.int32, (length, length), 0)
    col = lax.broadcasted_iota(jnp.int32, (length, length), 1)
    inclusive = row >= col
    strict = row > col
    diagonal = row == col
    ones_low = inclusive.astype(F32).astype(BF16)
    ones_up = (row <= col).astype(F32).astype(BF16)
    eye = diagonal.astype(F32).astype(BF16)
    picked = [gates[chunk, e] for e in ids]
    g_narrow = jnp.concatenate([gate[0:2] for gate in picked], axis=0).astype(BF16)
    b_narrow = jnp.concatenate([gate[2:4] for gate in picked], axis=0).astype(BF16)
    g_col = dot_nt(ones_low, g_narrow)
    g_row = dot(g_narrow, ones_up)
    b = dot_nt(eye, b_narrow)
    lane = lax.broadcasted_iota(jnp.int32, (BASE, length), 1)
    sub = lax.broadcasted_iota(jnp.int32, (BASE, length), 0)
    parts = length // BASE
    unit_cols = []
    compact = []
    for m, e in enumerate(ids):
        q = q_heads[chunk, e]
        k = k_heads[chunk, e]
        both = dot_nt(jnp.concatenate([k, q], axis=0), k)
        kk = both[:length]
        qk = both[length:]
        squares = jnp.where(diagonal, kk, 0.0)
        n_row = lax.rsqrt(jnp.sum(squares, axis=0, keepdims=True) + norm_epsilon)
        n_col = lax.rsqrt(jnp.sum(squares, axis=1, keepdims=True) + norm_epsilon)
        unit_cols += [n_col, n_col]
        kk = kk * n_row * n_col
        qk = qk * n_row
        for r in range(2):
            h = 2 * m + r
            decay = jnp.exp(jnp.where(inclusive, g_col[:, h:h + 1] - g_row[h:h + 1, :], 0.0))
            m_ref[group, h] = jnp.where(inclusive, qk * decay, 0.0)
            a = jnp.where(strict, kk * decay * b[:, h:h + 1], 0.0)
            a_rows[h] = a
            piece = jnp.zeros((BASE, length), F32)
            for p in range(parts):
                piece = jnp.where(lane // BASE == p, a[p * BASE:(p + 1) * BASE], piece)
            compact.append(piece)
    inverses = [(lane % BASE == sub).astype(F32) for _ in range(value_heads)]
    for j in range(BASE - 1):
        index = (lane // BASE) * BASE + j
        for h in range(value_heads):
            factor = jnp.take_along_axis(compact[h], index, axis=1)
            inverses[h] = inverses[h] - factor * inverses[h][j:j + 1, :]
    block_masks = [lane // BASE == p for p in range(parts)]
    levels = []
    size = BASE
    while size < length:
        levels.append((size, range(size, length, 2 * size)))
        size *= 2
    heads = range(value_heads)
    for h in heads:
        blocks = [jnp.where(block_masks[p], inverses[h], 0.0) for p in range(parts)]
        t_ref[group, h] = jnp.concatenate(blocks, axis=0)
    for size, starts in levels:
        columns = lax.broadcasted_iota(jnp.int32, (size, length), 1) // size
        empty = jnp.zeros((size, length), F32)
        steps = []
        for h in heads:
            lower = [
                jnp.where(columns == start // size - 1, a_rows[h, start:start + size, :], 0.0)
                for start in starts
            ]
            steps.append(dot3(jnp.concatenate(lower, axis=0), t_ref[group, h]))
        for h in heads:
            spread = []
            for n in range(len(starts)):
                spread += [empty, steps[h][n * size:(n + 1) * size]]
            odd = jnp.concatenate(
                [t_ref[group, h, start:start + size, :] for start in starts], axis=0
            )
            odd = odd - dot3(odd, jnp.concatenate(spread, axis=0))
            for n, start in enumerate(starts):
                t_ref[group, h, start:start + size, :] = odd[n * size:(n + 1) * size]
    units = jnp.concatenate(unit_cols, axis=1)
    growth = jnp.exp(g_col)
    rest = jnp.exp(g_col[length - 1:length, :] - g_col) * units
    aux_ref[group] = jnp.concatenate([growth, b, b * growth * units, rest], axis=1)


def advance_group(group, chunk, ids, lives, owners, slots, q_heads, k_heads, v_heads, t_ref, m_ref,
                  aux_ref, gain, states, stage, o_rows):
    length, key_dim = q_heads.shape[2:]
    width = v_heads.shape[-1]
    value_heads = 2 * len(ids)
    all_heads = 2 * q_heads.shape[0]
    aux = aux_ref[group]
    columns = lambda n, h: aux[:, n * value_heads + h:n * value_heads + h + 1]
    half = lambda pair, r: pair[:, r * width:(r + 1) * width]
    token = lax.broadcasted_iota(jnp.int32, (length, width), 0)
    keys, applied = [], []
    for m, e in enumerate(ids):
        q = q_heads[chunk, e]
        k = k_heads[chunk, e]
        s_high, s_low = split(states[owners[m], slots[m]])
        kq = jnp.concatenate([k, q], axis=0)
        keys.append(k)
        applied.append(
            dot(jnp.concatenate([kq, kq], axis=1), jnp.concatenate([s_high, s_low], axis=0))
        )
    fixed = []
    for h in range(value_heads):
        v = v_heads[chunk, ids[h // 2], h % 2].astype(F32)
        right = columns(1, h) * v - columns(2, h) * half(applied[h // 2][:length], h % 2)
        fixed.append(dot3(t_ref[group, h], right))
    powers = []
    for m, e in enumerate(ids):
        k = keys[m]
        update = jnp.concatenate(
            [columns(3, 2 * m + r) * fixed[2 * m + r] for r in range(2)], axis=1
        )
        u_high, u_low = split(update)
        added = dot_tn(jnp.concatenate([k, k], axis=0), jnp.concatenate([u_high, u_low], axis=0))
        state = states[owners[m], slots[m]]
        later = []
        for r in range(2):
            last = aux[length - 1:length, 2 * m + r:2 * m + r + 1]
            later.append(last * half(state, r) + half(added, r))
        word, pair_powers = code_pair(later)
        stage[chunk, group, m * key_dim:(m + 1) * key_dim, :] = word
        powers.append(pair_powers)
    stage[chunk, group, len(ids) * key_dim:, :] = jnp.concatenate(powers, axis=0)
    for h in range(value_heads):
        out = columns(0, h) * half(applied[h // 2][length:], h % 2)
        out = out + dot3(m_ref[group, h], fixed[h])
        mean_square = jnp.mean(out * out, axis=1, keepdims=True)
        normed = out * lax.rsqrt(mean_square + norm_epsilon) * gain
        rows = pl.ds(2 * chunk + h % 2, length, stride=all_heads)
        o_rows[group * len(ids) + h // 2, rows, :] = jnp.where(token < lives[h // 2], normed, 0.0)


def exchange_kernel(order_ref, owner_ref, slot_ref, count_ref, gain_ref, g_ref, b_ref, q_any, k_any,
                    v_any, parents_any, mixed, codes, early, parents, q_raw, k_raw, v_raw, q_rows,
                    k_rows, v_rows, q_heads, k_heads, v_heads, gates, t_ref, m_ref, aux_ref, a_rows,
                    blocks, scales, states, stage, o_rows, first_sem, parent_sem, raw_sem, line_send,
                    line_recv, final_send, final_recv):
    ring = lax.axis_size("seq")
    me = lax.axis_index("seq")
    chunks, expansions = q_heads.shape[:2]
    groups = ring
    depth = q_raw.shape[0]
    per_peer = expansions // ring

    def parent_copy(c):
        return pltpu.make_async_copy(
            parents_any.at[:, 2 * c:2 * c + 2], parents.at[c], parent_sem.at[c]
        )

    def raw_copies(e):
        pairs = ((q_any, q_raw), (k_any, k_raw), (v_any, v_raw))
        slot = lax.rem(e, depth)
        return [
            pltpu.make_async_copy(a.at[e], b.at[slot], raw_sem.at[slot, n])
            for n, (a, b) in enumerate(pairs)
        ]

    def line_copies(c, way, hop, source, peer):
        return [
            pltpu.make_async_remote_copy(
                src_ref=held.at[c, source],
                dst_ref=held.at[c, source],
                send_sem=line_send.at[c, way, hop, n],
                recv_sem=line_recv.at[c, way, hop, n],
                device_id={"seq": peer},
                device_id_type=MESH,
            )
            for n, held in enumerate((scales, blocks))
        ]

    def first_copy(i):
        return pltpu.make_async_copy(
            parents_any.at[i, 0:2], parents.at[0, i], first_sem.at[i]
        )

    def first_send(i):
        if i == 0:
            pl.semaphore_wait(barrier, ring - 1)
        held = blocks.at[0, me, i] if i < blocks.shape[2] else scales.at[0, me]
        kind = 1 if i < blocks.shape[2] else 0
        for way, step in ((0, 1), (1, -1)):
            @pl.when((me + step >= 0) & (me + step <= ring - 1))
            def _():
                pltpu.make_async_remote_copy(
                    src_ref=held,
                    dst_ref=held,
                    send_sem=line_send.at[0, way, 0, kind],
                    recv_sem=line_recv.at[0, way, 0, kind],
                    device_id={"seq": me + step},
                    device_id_type=MESH,
                ).start()

    def line_start(c):
        @pl.when(me < ring - 1)
        def _():
            for copy in line_copies(c, 0, 0, me, me + 1):
                copy.start()

        @pl.when(me > 0)
        def _():
            for copy in line_copies(c, 1, 0, me, me - 1):
                copy.start()

    def line_hop(c, hop):
        for way, step in ((0, 1), (1, -1)):
            source = me - step * hop
            inside = (source >= 0) & (source <= ring - 1)
            onward = inside & (me + step >= 0) & (me + step <= ring - 1)

            @pl.when(inside)
            def _():
                for copy in line_copies(c, way, hop - 1, source, me - step):
                    copy.wait_recv()

            @pl.when(onward)
            def _():
                for copy in line_copies(c, way, hop, source, me + step):
                    copy.start()

    def line_drain(c, hop):
        for way, step in ((0, 1), (1, -1)):
            source = me - step * hop
            inside = (source >= 0) & (source <= ring - 1)
            onward = inside & (me + step >= 0) & (me + step <= ring - 1)

            @pl.when(onward)
            def _():
                for copy in line_copies(c, way, hop, source, me + step):
                    copy.wait_send()

    def final_copy(c, i, source, peer):
        return pltpu.make_async_remote_copy(
            src_ref=stage.at[c, i],
            dst_ref=codes.at[c, source],
            send_sem=final_send.at[c, i],
            recv_sem=final_recv.at[c, i],
            device_id={"seq": peer},
            device_id_type=MESH,
        )

    def own_copy(c):
        return pltpu.make_async_copy(
            stage.at[c, groups - 1], codes.at[c, me], final_send.at[c, groups - 1]
        )

    def members(i):
        first = lax.rem(me + turn(ring, i), ring) * expansions + me * per_peer
        return [order_ref[first + a] for a in range(per_peer)]

    for i in range(blocks.shape[2]):
        first_copy(i).start()
    barrier = pltpu.get_barrier_semaphore()
    for i in range(1, ring):
        pl.semaphore_signal(
            barrier, inc=1, device_id={"seq": lax.rem(me + i, ring)}, device_id_type=MESH
        )
    encode_chunk(parents, blocks, scales, 0, me, lambda i: first_copy(i).wait(), first_send)
    first_send(blocks.shape[2])
    for c in range(1, chunks):
        parent_copy(c).start()

    @pl.loop(0, depth)
    def _(e):
        for copy in raw_copies(e):
            copy.start()

    for c in range(1, chunks):
        parent_copy(c).wait()
        encode_chunk(parents, blocks, scales, c, me)
        if c == 1:
            line_start(1)

    @pl.loop(0, expansions)
    def _(e):
        for copy in raw_copies(e):
            copy.wait()
        unpack_expansion(e, lax.rem(e, depth), count_ref[me * expansions + e], q_raw, k_raw, v_raw, g_ref, b_ref,
                         q_rows, k_rows, v_rows, q_heads, k_heads, v_heads, gates)

        @pl.when(e + depth < expansions)
        def _():
            for copy in raw_copies(e + depth):
                copy.start()

    line_hop(0, 1)
    gain = gain_ref[...].astype(F32)

    @pl.loop(0, chunks)
    def _(c):
        def tick(t):
            @pl.when(c + 1 < chunks)
            def _():
                @pl.when((t == 2) & (c + 2 < chunks))
                def _():
                    line_start(c + 2)

                @pl.when((t > 1) & (t % 2 == 1) & (t // 2 < ring - 1))
                def _():
                    line_hop(c + 1, t // 2)

        @pl.loop(0, groups)
        def _(i):
            tick(i)

            @pl.when((c == 0) & (i > 2) & (i < ring))
            def _():
                line_hop(0, i - 1)

            ids = [jnp.maximum(number - me * expansions, 0) for number in members(i)]
            prepare_group(i, c, ids, q_heads, k_heads, gates, t_ref, m_ref, aux_ref, a_rows)

        line_hop(c, ring - 1)

        @pl.loop(0, ring)
        def _(source):
            decode_chunk(c, source, blocks, scales, states)

        @pl.loop(0, groups)
        def _(i):
            tick(groups + i)
            numbers = members(i)
            ids = [jnp.maximum(number - me * expansions, 0) for number in numbers]
            lives = [count_ref[number] for number in numbers]
            owners = [owner_ref[number] for number in numbers]
            slots = [slot_ref[number] for number in numbers]
            advance_group(i, c, ids, lives, owners, slots, q_heads, k_heads, v_heads, t_ref, m_ref,
                          aux_ref, gain, states, stage, o_rows)

            @pl.when(i < groups - 1)
            def _():
                final_copy(c, i, me, lax.rem(me + turn(ring, i), ring)).start()

            @pl.when(i == groups - 1)
            def _():
                own_copy(c).start()

    @pl.loop(0, expansions)
    def _(e):
        row = 0
        for i in range(groups):
            for a, number in enumerate(members(i)):
                here = number == me * expansions + e
                row = jnp.maximum(row, jnp.where(here, i * per_peer + a, 0))
        mixed[e] = o_rows[row].astype(BF16)

    @pl.loop(0, chunks)
    def _(c):
        own_copy(c).wait()

        @pl.loop(0, ring - 1)
        def _(hop):
            line_drain(c, hop)

        @pl.loop(0, groups - 1)
        def _(i):
            source = lax.rem(me + ring - turn(ring, i), ring)
            copy = final_copy(c, i, source, lax.rem(me + turn(ring, i), ring))
            copy.wait_send()
            copy.wait_recv()

            @pl.when(c < chunks - 1)
            def _():
                decode_finals(codes.at[c, source], early, source * per_peer, 2 * c)

        @pl.when(c < chunks - 1)
        def _():
            decode_finals(codes.at[c, me], early, me * per_peer, 2 * c)


def exchange(order, owner, slot, count, gain, decay, rate, queries, keys, values, parents, ring):
    expansions, rows, key_dim = queries.shape
    cached, value_heads, _, width = parents.shape
    chunks = value_heads // 2
    length = rows // chunks
    per_peer = expansions // ring
    heads = 2 * per_peer
    depth = min(RAW_SLOTS, expansions)
    final_rows = per_peer * (key_dim + 1)
    anywhere = pl.BlockSpec(memory_space=pl.ANY)
    whole = pl.BlockSpec(memory_space=pltpu.VMEM)
    scalars = pl.BlockSpec(memory_space=pltpu.SMEM)
    work = expansions * value_heads
    return pl.pallas_call(
        exchange_kernel,
        out_shape=(
            pltpu.VMEM(values.shape, BF16),
            pltpu.VMEM((chunks, ring, final_rows, width), jnp.int32),
            pltpu.VMEM((expansions, value_heads - 2, key_dim, width), F32),
        ),
        in_specs=[scalars] * 4 + [whole] * 3 + [anywhere] * 4,
        out_specs=(whole, whole, whole),
        scratch_shapes=[
            pltpu.VMEM((chunks, cached, 2, key_dim, width), F32),
            pltpu.VMEM((depth,) + queries.shape[1:], BF16),
            pltpu.VMEM((depth,) + keys.shape[1:], BF16),
            pltpu.VMEM((depth,) + values.shape[1:], BF16),
            pltpu.VMEM((rows, key_dim), F32),
            pltpu.VMEM((rows, key_dim), F32),
            pltpu.VMEM((length * value_heads, width), F32),
            pltpu.VMEM((chunks, expansions, length, key_dim), BF16),
            pltpu.VMEM((chunks, expansions, length, key_dim), BF16),
            pltpu.VMEM((chunks, expansions, 2, length, width), BF16),
            pltpu.VMEM((chunks, expansions, 8, length), F32),
            pltpu.VMEM((ring, heads, length, length), F32),
            pltpu.VMEM((ring, heads, length, length), F32),
            pltpu.VMEM((ring, length, 4 * heads), F32),
            pltpu.VMEM((heads, length, length), F32),
            pltpu.VMEM((chunks, ring, cached, key_dim, width), jnp.int32),
            pltpu.VMEM((chunks, ring, cached, width), jnp.int32),
            pltpu.VMEM((ring, cached, key_dim, 2 * width), F32),
            pltpu.VMEM((chunks, ring, final_rows, width), jnp.int32),
            pltpu.VMEM(values.shape, F32),
            pltpu.SemaphoreType.DMA((cached,)),
            pltpu.SemaphoreType.DMA((chunks,)),
            pltpu.SemaphoreType.DMA((depth, 3)),
            pltpu.SemaphoreType.DMA((chunks, 2, ring - 1, 2)),
            pltpu.SemaphoreType.DMA((chunks, 2, ring - 1, 2)),
            pltpu.SemaphoreType.DMA((chunks, ring)),
            pltpu.SemaphoreType.DMA((chunks, ring)),
        ],
        compiler_params=pltpu.CompilerParams(
            vmem_limit_bytes=EXCHANGE_BYTES, collective_id=0, has_side_effects=True
        ),
        cost_estimate=pl.CostEstimate(
            flops=work * 40 * length**3,
            bytes_accessed=work * length**2 * 16,
            transcendentals=work * length**2,
        ),
        name="exchange",
    )(order, owner, slot, count, gain, decay, rate, queries, keys, values, parents)


def finish_kernel(mixed_ref, codes_ref, early_ref, final_any, mixed_any, late, mixed_sem, early_sem,
                  late_sem):
    chunks, ring = codes_ref.shape[:2]
    per_peer = late.shape[0] // ring
    head = early_ref.shape[1]
    group = lambda source: pl.ds(source * per_peer, per_peer)
    copies = [pltpu.make_async_copy(mixed_ref, mixed_any, mixed_sem)]
    for source in range(ring):
        copies.append(
            pltpu.make_async_copy(
                early_ref.at[group(source)],
                final_any.at[group(source), 0:head],
                early_sem.at[source],
            )
        )
    for copy in copies:
        copy.start()
    for source in range(ring):
        decode_finals(codes_ref.at[chunks - 1, source], late, source * per_peer, 0)
        copy = pltpu.make_async_copy(
            late.at[group(source)], final_any.at[group(source), head:head + 2], late_sem.at[source]
        )
        copy.start()
        copies.append(copy)
    for copy in copies:
        copy.wait()


def finish(mixed, codes, early, ring):
    expansions, early_heads, key_dim, width = early.shape
    whole = pl.BlockSpec(memory_space=pltpu.VMEM)
    anywhere = pl.BlockSpec(memory_space=pl.ANY)
    return pl.pallas_call(
        finish_kernel,
        out_shape=(
            jax.ShapeDtypeStruct((expansions, early_heads + 2, key_dim, width), F32),
            jax.ShapeDtypeStruct(mixed.shape, BF16),
        ),
        in_specs=[whole, whole, whole],
        out_specs=(anywhere, anywhere),
        scratch_shapes=[
            pltpu.VMEM((expansions, 2, key_dim, width), F32),
            pltpu.SemaphoreType.DMA,
            pltpu.SemaphoreType.DMA((ring,)),
            pltpu.SemaphoreType.DMA((ring,)),
        ],
        compiler_params=pltpu.CompilerParams(vmem_limit_bytes=FINISH_BYTES),
        name="finish",
    )(*[pltpu.with_memory_space_constraint(x, pltpu.VMEM) for x in (mixed, codes, early)])


def shards(queries, keys, values, log_decay, write_rate, norm_gain, parent_cache, order,
           parent_owner, parent_slot, token_count):
    ring = lax.axis_size("seq")
    expansions, length, key_heads, key_dim = queries.shape
    value_heads = 2 * key_heads
    width = values.shape[-1]
    cached = parent_cache.shape[0]
    turned = lambda x: x.transpose(0, 2, 3, 1).reshape(expansions, value_heads, length)
    mixed, codes, early = exchange(
        order,
        parent_owner,
        parent_slot,
        token_count,
        norm_gain.reshape(1, width),
        turned(log_decay),
        turned(write_rate),
        queries.reshape(expansions, length * key_heads, key_dim),
        keys.reshape(expansions, length * key_heads, key_dim),
        values.reshape(expansions, length * value_heads, width),
        parent_cache.reshape(cached, value_heads, key_dim, width),
        ring,
    )
    final, mixed = finish(mixed, codes, early, ring)
    return (
        mixed.reshape(values.shape),
        final.reshape((expansions,) + parent_cache.shape[1:]),
    )


def solution(mesh):
    heads = ("head", "sub")
    rows = ("groups", "seq")
    placed = (
        P(rows, None, heads, None),
        P(rows, None, heads, None),
        P(rows, None, heads, None, None),
        P(rows, None, heads, None),
        P(rows, None, heads, None),
        P(),
        P(rows, heads, None, None, None),
        P("groups"),
        P("groups"),
        P("groups"),
        P("groups"),
    )
    return jax.shard_map(
        shards,
        mesh=mesh,
        in_specs=placed,
        out_specs=(P(rows, None, heads, None, None), P(rows, heads, None, None, None)),
        check_vma=False,
    )
```
